32 devices in a mesh: dap: 8 (over y, x, core), seq: 4 (over z).
Axes of the slice: x: 2, y: 2, z: 4, core: 2. Of those that a mesh axis runs over, the one named last changes fastest.
Arguments:
- homolog_tensor: bfloat16 [8, 32, 256], P('dap', 'seq'), may hold values from -6 to 6
- pair_features: bfloat16 [32, 32, 128], P('seq', 'dap'), may hold values from -6 to 6
- entry_real_mask: int32 [8, 32], P('dap', 'seq'), may hold values 0 or 1
- chain_ids: int32 [32], replicated, may hold values from 0 to 3, never falling along the last dimension, each value on 1 to 16 neighbouring positions
- horizontal_matrices: bfloat16 [256, 1024], replicated, may hold values from -0.375 to 0.375
- horizontal_projector: bfloat16 [256, 256], replicated, may hold values from -0.375 to 0.375
- bias_proj: float32 [128, 8], replicated, may hold values from -35.35534 to 35.35534
- chain_bias: float32 [2, 8], replicated, may hold values from -4 to 4
- column_proj: bfloat16 [256, 1024], replicated, may hold values from -12.5 to 12.5
- vertical_projector: bfloat16 [256, 256], replicated, may hold values from -0.375 to 0.375
- expansion_matrix: bfloat16 [256, 1024], replicated, may hold values from -0.375 to 0.375
- contraction_matrix: bfloat16 [1024, 256], replicated, may hold values from -0.1875 to 0.1875
Outputs:
- updated: bfloat16 [8, 32, 256], P('dap', 'seq')
The draws below stay inside these ranges and needn't reach their ends.
Inputs may be any that keep to these rules, and one draw needn't show every extreme that they name: `chain_ids`: chain numbers never fall along the residues.
All inputs are finite; a program needn't handle non-finite values. No bound on the sum of `entry_real_mask` on one device may be relied on, other than what follows from the above.
Results may differ from the reference program's by a relative error of at most 0.013.
The reference program's roundings to bfloat16 on the way count: a program that leaves them out, or rounds other values in their place, can miss the bound.
Values may be sent and summed in bfloat16 or wider, within the bound.
No kernel may reach another device: no remote copies, remote signals or barrier semaphores. Data moves between devices by JAX's collectives and lax.ppermute only.
A program may use at most 64 MiB of HBM per device.

```python
import math
import jax
import jax.numpy as jnp
import numpy as np
from jax import lax

FEATURE_DEPTH = 256
CZ = 128
HEAD_TOTAL = 8
HEAD_DEPTH = 32
EXPANDED_UNITS = 1024
HOMOLOG_COUNT = 8
ASSEMBLY_SITES = 32


def draw_bias_proj(key, part):
    starting_tensor = jnp.clip(jax.random.normal(jax.random.fold_in(key, 11), (CZ, HEAD_TOTAL), jnp.float32), -5.0, 5.0) * CZ ** (-0.5)
    return starting_tensor


def draw_column_proj(key, part):
    expanded_dimension = HEAD_TOTAL * HEAD_DEPTH
    starting_tensor = jnp.clip(jax.random.normal(jax.random.fold_in(key, 21), (FEATURE_DEPTH, 4 * expanded_dimension), jnp.float32), -5.0, 5.0) * FEATURE_DEPTH ** (-0.5)
    return starting_tensor.astype(jnp.bfloat16)


def touch_ends(array, rng, smallest, top_value):
    index_at = [jax.random.randint(jax.random.fold_in(rng, axis), (), 0, length) for axis, length in enumerate(array.shape)]
    main_axis = array.shape.index(max(array.shape))
    next_to = index_at[:main_axis] + [(index_at[main_axis] + 1) % array.shape[main_axis]] + index_at[main_axis + 1:]
    return array.at[tuple(index_at)].set(smallest).at[tuple(next_to)].set(top_value)


def block_levels(key, dims, split, least, high):
    loudness, own = 1.0, jax.random.fold_in(key, 6)
    for position, parts in split:
        steps = jnp.exp(jax.random.uniform(jax.random.fold_in(own, position), (parts,), jnp.float32, least / len(split), high / len(split)))
        loudness = loudness * jnp.repeat(steps, dims[position] // parts).reshape([-1 if axis == position else 1 for axis in range(len(dims))])
    return loudness


def profile(amount, total, bound, lean):
    weights = [(1 << 20) // math.isqrt(rank ** lean) + 1 for rank in range(2, amount + 1)]
    spare, holding = total - bound - (amount - 1), [1] * (amount - 1)
    while spare > 0:
        free = [i for i in range(amount - 1) if holding[i] < bound]
        whole, left = sum([weights[i] for i in free]), spare
        for i in free:
            addition = min(bound - holding[i], max(1, left * weights[i] // whole), spare)
            holding[i] = holding[i] + addition
            spare = spare - addition
    return np.array([bound] + holding)


def uneven(stream_key, amount, total, limit, slope):
    if amount == 2:
        one = jax.random.randint(stream_key, (), max(1, total - limit), min(limit, total - 1) + 1)
        return jnp.stack([one, total - one])
    lengths = jnp.asarray(profile(amount, total, limit, slope), jnp.int32)
    pairs = (amount - 1) // 2
    giver, taker = lengths[1:1 + 2 * pairs:2], lengths[2:2 + 2 * pairs:2]
    room = jnp.minimum(giver - 1, limit - taker)
    shifted = jax.random.randint(jax.random.fold_in(stream_key, 1), (pairs,), 0, 1 << 20) % (room + 1)
    lengths = lengths.at[1:1 + 2 * pairs:2].set(giver - shifted).at[2:2 + 2 * pairs:2].set(taker + shifted)
    return lengths[jax.random.permutation(jax.random.fold_in(stream_key, 2), amount)]


def centred(stream_key, dims, scale, limit, pieces=(), kind=jnp.bfloat16):
    gain = block_levels(stream_key, dims, pieces, -0.22, 0.18) if pieces else 1.0
    array = jax.random.normal(stream_key, dims, jnp.float32) * scale * gain
    return jnp.minimum(jnp.maximum(array, -limit), limit).astype(kind)


def setup_inputs(seed: int = 0) -> dict:
    splits = jax.random.split(jax.random.key(seed), 13)
    homolog_tensor = centred(splits[0], (HOMOLOG_COUNT, ASSEMBLY_SITES, FEATURE_DEPTH), 1.0, 6.0, ((0, 8), (1, 4)))
    pair_features = centred(splits[1], (ASSEMBLY_SITES, ASSEMBLY_SITES, CZ), 1.0, 6.0, ((0, 4), (1, 8)))
    entry_real_mask = touch_ends((jax.random.randint(splits[2], (HOMOLOG_COUNT, ASSEMBLY_SITES), 0, 8) < 7).astype(jnp.int32), jax.random.fold_in(splits[2], 1), 0, 1)
    chain_ids = jnp.searchsorted(jnp.cumsum(uneven(splits[3], 4, ASSEMBLY_SITES, ASSEMBLY_SITES // 2, 0)), jnp.arange(ASSEMBLY_SITES), side="right").astype(jnp.int32)
    horizontal_matrices = centred(splits[4], (FEATURE_DEPTH, 4 * HEAD_TOTAL * HEAD_DEPTH), FEATURE_DEPTH ** -0.5, 0.375)
    horizontal_projector = centred(splits[5], (HEAD_TOTAL * HEAD_DEPTH, FEATURE_DEPTH), (HEAD_TOTAL * HEAD_DEPTH) ** -0.5, 0.375)
    bias_proj = draw_bias_proj(jax.random.fold_in(splits[12], 71), 0)
    chain_bias = centred(splits[7], (2, HEAD_TOTAL), 1.0, 4.0, (), jnp.float32)
    column_proj = draw_column_proj(jax.random.fold_in(splits[12], 71), 0)
    vertical_projector = centred(splits[9], (HEAD_TOTAL * HEAD_DEPTH, FEATURE_DEPTH), (HEAD_TOTAL * HEAD_DEPTH) ** -0.5, 0.375)
    expansion_matrix = centred(splits[10], (FEATURE_DEPTH, EXPANDED_UNITS), FEATURE_DEPTH ** -0.5, 0.375)
    contraction_matrix = centred(splits[11], (EXPANDED_UNITS, FEATURE_DEPTH), EXPANDED_UNITS ** -0.5, 0.1875)
    return dict(homolog_tensor=homolog_tensor, pair_features=pair_features, entry_real_mask=entry_real_mask, chain_ids=chain_ids, horizontal_matrices=horizontal_matrices, horizontal_projector=horizontal_projector, bias_proj=bias_proj, chain_bias=chain_bias, column_proj=column_proj, vertical_projector=vertical_projector, expansion_matrix=expansion_matrix, contraction_matrix=contraction_matrix)


epsilon = 1e-05

def layer_norm(inputs):
    center = inputs - lax.optimization_barrier(jnp.mean(inputs, axis=-1, keepdims=True))
    spread = lax.optimization_barrier(jnp.mean(center * center, axis=-1, keepdims=True))
    return center * lax.rsqrt(spread + epsilon)

def attend(queries, key_part, value_part, keep_mask, bias_term):
    scores = jnp.einsum('ihd,jhd->hij', queries.astype(jnp.float32), key_part.astype(jnp.float32)) * HEAD_DEPTH ** (-0.5)
    if bias_term is not None:
        scores = scores + bias_term.astype(jnp.float32)
    scores = jnp.where(keep_mask[None, None, :] > 0, scores, -1000000000.0)
    weights = jax.nn.softmax(scores, axis=-1).astype(jnp.bfloat16)
    return jnp.einsum('hij,jhd->ihd', weights.astype(jnp.float32), value_part.astype(jnp.float32))

def column_update(column, keep_column, column_proj, vertical_projector, expansion_matrix, contraction_matrix):
    expanded_dimension = HEAD_TOTAL * HEAD_DEPTH
    standardized = layer_norm(column.astype(jnp.float32)).astype(jnp.bfloat16)
    projected = jnp.dot(standardized, column_proj, preferred_element_type=jnp.float32).astype(jnp.bfloat16)
    queries = projected[:, :expanded_dimension].reshape(-1, HEAD_TOTAL, HEAD_DEPTH)
    key_part = projected[:, expanded_dimension:2 * expanded_dimension].reshape(-1, HEAD_TOTAL, HEAD_DEPTH)
    value_part = projected[:, 2 * expanded_dimension:3 * expanded_dimension].reshape(-1, HEAD_TOTAL, HEAD_DEPTH)
    attended = attend(queries, key_part, value_part, keep_column, None).reshape(-1, expanded_dimension)
    sigmoid_scaled = (jax.nn.sigmoid(projected[:, 3 * expanded_dimension:].astype(jnp.float32)) * attended).astype(jnp.bfloat16)
    mixed = column.astype(jnp.float32) + jnp.dot(sigmoid_scaled, vertical_projector, preferred_element_type=jnp.float32)
    inner = jnp.maximum(jnp.dot(layer_norm(mixed).astype(jnp.bfloat16), expansion_matrix, preferred_element_type=jnp.float32), 0.0).astype(jnp.bfloat16)
    return (mixed + jnp.dot(inner, contraction_matrix, preferred_element_type=jnp.float32)).astype(jnp.bfloat16)

def reference(homolog_tensor, pair_features, entry_real_mask, chain_ids, horizontal_matrices, horizontal_projector, bias_proj, chain_bias, column_proj, vertical_projector, expansion_matrix, contraction_matrix):
    expanded_dimension = HEAD_TOTAL * HEAD_DEPTH
    normed_pair = layer_norm(pair_features.astype(jnp.float32))
    projected_pair = jnp.einsum('ijc,ch->hij', normed_pair, bias_proj, precision=lax.Precision.HIGHEST)
    same_chain = (chain_ids[:, None] == chain_ids[None, :]).astype(jnp.float32)
    chain_term = chain_bias[0][:, None, None] * same_chain + chain_bias[1][:, None, None] * (1.0 - same_chain)
    pair_bias = (projected_pair + chain_term).astype(jnp.bfloat16)
    standardized = layer_norm(homolog_tensor.astype(jnp.float32)).astype(jnp.bfloat16)
    horizontal_quadruple = jnp.dot(standardized.reshape(-1, FEATURE_DEPTH), horizontal_matrices, preferred_element_type=jnp.float32).astype(jnp.bfloat16).reshape(HOMOLOG_COUNT, ASSEMBLY_SITES, 4 * expanded_dimension)

    def one_row(inputs_row):
        row_values, row_keep = inputs_row
        queries = row_values[:, :expanded_dimension].reshape(ASSEMBLY_SITES, HEAD_TOTAL, HEAD_DEPTH)
        key_part = row_values[:, expanded_dimension:2 * expanded_dimension].reshape(ASSEMBLY_SITES, HEAD_TOTAL, HEAD_DEPTH)
        value_part = row_values[:, 2 * expanded_dimension:3 * expanded_dimension].reshape(ASSEMBLY_SITES, HEAD_TOTAL, HEAD_DEPTH)
        return attend(queries, key_part, value_part, row_keep, pair_bias).reshape(ASSEMBLY_SITES, expanded_dimension)
    attended = lax.map(one_row, (horizontal_quadruple, entry_real_mask))
    sigmoid_scaled = (jax.nn.sigmoid(horizontal_quadruple[..., 3 * expanded_dimension:].astype(jnp.float32)) * attended).astype(jnp.bfloat16)
    leading_homolog = (homolog_tensor.astype(jnp.float32) + jnp.dot(sigmoid_scaled.reshape(-1, expanded_dimension), horizontal_projector, preferred_element_type=jnp.float32).reshape(HOMOLOG_COUNT, ASSEMBLY_SITES, FEATURE_DEPTH)).astype(jnp.bfloat16)

    def single_column(inputs_col):
        return column_update(inputs_col[0], inputs_col[1], column_proj, vertical_projector, expansion_matrix, contraction_matrix)
    output_list = lax.map(single_column, (jnp.swapaxes(leading_homolog, 0, 1), jnp.swapaxes(entry_real_mask, 0, 1)))
    return jnp.swapaxes(output_list, 0, 1)
```

```python
import jax
import jax.numpy as jnp
from jax import lax
from jax.experimental import pallas as pl
from jax.experimental.pallas import tpu as pltpu
from jax.sharding import PartitionSpec as P

HEAD_TOTAL = 8
HEAD_DEPTH = 32


epsilon = 1e-05


def layer_norm(inputs):
    center = inputs - jnp.mean(inputs, axis=-1, keepdims=True)
    spread = jnp.mean(center * center, axis=-1, keepdims=True)
    return center * lax.rsqrt(spread + epsilon)


def attend(queries, key_part, value_part, keep_mask, bias_term):
    scores = jnp.einsum(
        "ihd,jhd->hij", queries, key_part, preferred_element_type=jnp.float32
    ) * HEAD_DEPTH ** (-0.5)
    if bias_term is not None:
        scores = scores + bias_term.astype(jnp.float32)
    scores = jnp.where(keep_mask[None, None, :] > 0, scores, -1000000000.0)
    weights = jax.nn.softmax(scores, axis=-1).astype(jnp.bfloat16)
    return jnp.einsum("hij,jhd->ihd", weights, value_part, preferred_element_type=jnp.float32)


def column_update(
    column, keep_column, column_proj, vertical_projector, expansion_matrix, contraction_matrix
):
    expanded_dimension = HEAD_TOTAL * HEAD_DEPTH
    standardized = layer_norm(column.astype(jnp.float32)).astype(jnp.bfloat16)
    projected = jnp.dot(standardized, column_proj, preferred_element_type=jnp.float32).astype(
        jnp.bfloat16
    )
    queries = projected[:, :expanded_dimension].reshape(-1, HEAD_TOTAL, HEAD_DEPTH)
    key_part = projected[:, expanded_dimension : 2 * expanded_dimension].reshape(
        -1, HEAD_TOTAL, HEAD_DEPTH
    )
    value_part = projected[:, 2 * expanded_dimension : 3 * expanded_dimension].reshape(
        -1, HEAD_TOTAL, HEAD_DEPTH
    )
    attended = attend(queries, key_part, value_part, keep_column, None).reshape(
        -1, expanded_dimension
    )
    sigmoid_scaled = (
        jax.nn.sigmoid(projected[:, 3 * expanded_dimension :].astype(jnp.float32)) * attended
    ).astype(jnp.bfloat16)
    mixed = column.astype(jnp.float32) + jnp.dot(
        sigmoid_scaled, vertical_projector, preferred_element_type=jnp.float32
    )
    inner = jnp.maximum(
        jnp.dot(
            layer_norm(mixed).astype(jnp.bfloat16),
            expansion_matrix,
            preferred_element_type=jnp.float32,
        ),
        0.0,
    ).astype(jnp.bfloat16)
    return (mixed + jnp.dot(inner, contraction_matrix, preferred_element_type=jnp.float32)).astype(
        jnp.bfloat16
    )


def body(
    homolog_tensor,
    pair_features,
    entry_real_mask,
    chain_ids,
    horizontal_matrices,
    horizontal_projector,
    bias_proj,
    chain_bias,
    column_proj,
    vertical_projector,
    expansion_matrix,
    contraction_matrix,
):
    row_count, local_residues, channels = homolog_tensor.shape
    expanded_dimension = HEAD_TOTAL * HEAD_DEPTH
    dap_count = lax.axis_size("dap")
    pair_rows, pair_columns, pair_width = pair_features.shape
    normed_pair = layer_norm(pair_features.astype(jnp.float32))
    projected_pair = jnp.einsum(
        "ijc,ch->hij", normed_pair, bias_proj, precision=lax.Precision.HIGHEST
    )
    row_chain = lax.dynamic_slice_in_dim(chain_ids, lax.axis_index("seq") * pair_rows, pair_rows)
    column_chain = lax.dynamic_slice_in_dim(
        chain_ids, lax.axis_index("dap") * pair_columns, pair_columns
    )
    same_chain = (row_chain[:, None] == column_chain[None, :]).astype(jnp.float32)
    chain_term = chain_bias[0][:, None, None] * same_chain + chain_bias[1][:, None, None] * (
        1.0 - same_chain
    )
    local_bias = (projected_pair + chain_term).astype(jnp.bfloat16)
    pair_bias = lax.all_gather(local_bias, "dap", axis=2, tiled=True)
    standardized = layer_norm(homolog_tensor.astype(jnp.float32)).astype(jnp.bfloat16)
    flat = standardized.reshape(-1, channels)
    keep_mask = entry_real_mask.astype(jnp.bfloat16)
    projected = (
        jnp.dot(flat, horizontal_matrices, preferred_element_type=jnp.float32)
        .astype(jnp.bfloat16)
        .reshape(row_count, local_residues, 4 * expanded_dimension)
    )
    queries = projected[..., :expanded_dimension]
    gating = projected[..., 3 * expanded_dimension :]
    key_values, keep_all = (
        lax.all_gather(
            projected[..., expanded_dimension : 3 * expanded_dimension], "seq", axis=1, tiled=True
        ),
        lax.all_gather(keep_mask, "seq", axis=1, tiled=True),
    )

    def one_row(inputs_row):
        row_queries, row_pairs, row_keep = inputs_row
        key_part = row_pairs[:, :expanded_dimension].reshape(-1, HEAD_TOTAL, HEAD_DEPTH)
        value_part = row_pairs[:, expanded_dimension:].reshape(-1, HEAD_TOTAL, HEAD_DEPTH)
        return attend(
            row_queries.reshape(local_residues, HEAD_TOTAL, HEAD_DEPTH),
            key_part,
            value_part,
            row_keep,
            pair_bias,
        ).reshape(local_residues, expanded_dimension)

    attended = lax.map(one_row, (queries, key_values, keep_all))
    sigmoid_scaled = (jax.nn.sigmoid(gating.astype(jnp.float32)) * attended).astype(jnp.bfloat16)
    row_result = jnp.dot(
        sigmoid_scaled.reshape(-1, expanded_dimension),
        horizontal_projector,
        preferred_element_type=jnp.float32,
    ).reshape(row_count, local_residues, channels)
    updated_rows = (homolog_tensor.astype(jnp.float32) + row_result).astype(jnp.bfloat16)
    per_device = local_residues // dap_count
    blocks = updated_rows.reshape(row_count, dap_count, per_device, channels)
    keep_blocks = keep_mask.reshape(row_count, dap_count, per_device)

    def single_column(inputs_col):
        return column_update(
            inputs_col[0],
            inputs_col[1],
            column_proj,
            vertical_projector,
            expansion_matrix,
            contraction_matrix,
        )

    column_block = lax.all_to_all(blocks, "dap", split_axis=1, concat_axis=0, tiled=True)
    column_keep = lax.all_to_all(keep_blocks, "dap", split_axis=1, concat_axis=0, tiled=True)
    inputs_col = (jnp.moveaxis(column_block[:, 0], 1, 0), jnp.moveaxis(column_keep[:, 0], 1, 0))
    output_list = lax.map(single_column, inputs_col)
    mixed = jnp.moveaxis(output_list, 0, 1)[:, None]
    returned = lax.all_to_all(mixed, "dap", split_axis=0, concat_axis=1, tiled=True)
    return returned.reshape(row_count, local_residues, channels)


LANES = 128
SUBLANES = 8
WHOLE_BYTES = 1 << 20
F32 = jnp.float32
BF16 = jnp.bfloat16


def mm(a, b):
    return lax.dot_general(a, b, (((1,), (0,)), ((), ())), preferred_element_type=F32)


def iota(shape, axis):
    return lax.broadcasted_iota(jnp.int32, shape, axis)


def normalize(parts, width):
    total = parts[0]
    for part in parts[1:]:
        total = total + part
    mean = jnp.sum(total, axis=-1, keepdims=True) * (1.0 / width)
    center = [part - mean for part in parts]
    total = center[0] * center[0]
    for part in center[1:]:
        total = total + part * part
    scale = lax.rsqrt(jnp.sum(total, axis=-1, keepdims=True) * (1.0 / width) + epsilon)
    return [part * scale for part in center]


def halves(x):
    return [x[:, k : k + LANES] for k in range(0, x.shape[1], LANES)]


def normalize_rows(x):
    return jnp.concatenate(normalize(halves(x), x.shape[1]), axis=1).astype(BF16)


def pack_kernel(msa_ref, pair_ref, mask_ref, proj_ref, chain_ref, chain_bias_ref, out_ref):
    queries, keys, width = pair_ref.shape
    cells = HEAD_TOTAL * queries
    dap, seq = lax.axis_index("dap"), lax.axis_index("seq")
    odd = lax.rem(dap, 2)
    spread = (iota((HEAD_TOTAL, LANES), 1) % cells // queries == iota((HEAD_TOTAL, LANES), 0)).astype(F32)
    proj = lax.dot_general(
        proj_ref[...], spread, (((1,), (0,)), ((), ())),
        precision=lax.Precision.HIGHEST, preferred_element_type=F32,
    )
    pair = pair_ref[...].astype(F32)
    pair = jnp.concatenate([pair, pair], axis=1).reshape(queries * 2 * keys, width)
    normed = normalize([pair], width)[0]
    bias = lax.dot_general(
        normed, proj, (((1,), (0,)), ((), ())),
        precision=lax.Precision.HIGHEST, preferred_element_type=F32,
    ).reshape(queries, 2 * keys, LANES)
    own = iota(bias.shape, 2) % queries == iota(bias.shape, 0)
    bias = jnp.sum(jnp.where(own, bias, 0.0), axis=0)
    shape = bias.shape
    row, lane = iota(shape, 0), iota(shape, 1)
    key_chain, query_chain = jnp.zeros(shape, jnp.int32), jnp.zeros(shape, jnp.int32)
    for k in range(keys):
        key_chain = jnp.where(row % keys == k, chain_ref[dap * keys + k], key_chain)
    for k in range(queries):
        query_chain = jnp.where(lane % queries == k, chain_ref[seq * queries + k], query_chain)
    same, other = jnp.zeros(shape, F32), jnp.zeros(shape, F32)
    for h in range(HEAD_TOTAL):
        here = lane % cells // queries == h
        same = jnp.where(here, chain_bias_ref[0, h], same)
        other = jnp.where(here, chain_bias_ref[1, h], other)
    bias = bias + jnp.where(key_chain == query_chain, same, other)
    mask = jnp.zeros(shape, F32)
    for k in range(SUBLANES):
        mask = jnp.where(row == k, mask_ref[0, k].astype(F32), mask)
    upper = (lane >= cells).astype(jnp.int32)
    tail = jnp.where(upper != odd, bias, mask)
    block = jnp.concatenate([*halves(msa_ref[0].astype(F32)), tail], axis=0).astype(BF16)
    out_ref[...] = jnp.broadcast_to(block[None], out_ref.shape)


def block_kernel(
    seq_count, block_ref, row_proj_ref, row_out_ref, column_proj_ref, column_out_ref, expansion_ref,
    contraction_ref, out_ref, normed_ref, second_ref, one_ref,
):
    count, rows, _ = block_ref.shape
    own_rows = SUBLANES
    width = rows * LANES // own_rows - LANES
    parts = width // LANES
    members = count // seq_count
    residues = seq_count * own_rows
    heads, depth = HEAD_TOTAL, HEAD_DEPTH
    inner = heads * depth
    cells = heads * own_rows
    tokens = members * own_rows
    dap, seq = lax.axis_index("dap"), lax.axis_index("seq")
    scaling = depth**-0.5

    def part(ref_index, k):
        return block_ref[ref_index, k * own_rows : (k + 1) * own_rows, :].astype(F32)

    everything = slice(None)
    x = [part(everything, k).reshape(count * own_rows, LANES) for k in range(parts)]
    normed = jnp.concatenate(normalize(x, width), axis=1).astype(BF16)
    key_values = mm(normed, row_proj_ref[:, inner : 3 * inner]).astype(BF16)
    normed_ref[...] = normed.reshape(members, seq_count, own_rows, width)
    own = normed_ref[:, seq].reshape(tokens, width)
    queries = mm(own, row_proj_ref[:, :inner]).astype(BF16).astype(F32)
    gates = mm(own, row_proj_ref[:, 3 * inner :]).astype(BF16).astype(F32)

    head_of = (iota((heads, 1, inner), 2) // depth == iota((heads, 1, inner), 0)).astype(F32)
    spread = (queries.reshape(members, 1, own_rows, inner) * head_of[None]).reshape(
        members * cells, inner
    ).astype(BF16)

    shape = (own_rows, LANES)
    row, lane = iota(shape, 0), iota(shape, 1)
    lower = lane < cells
    tails = [
        [block_ref[m * seq_count + s, parts * own_rows :, :].astype(F32) for s in range(seq_count)]
        for m in range(members)
    ]
    bias = []
    for m in range(0, members, 2):
        even = block_ref[m * seq_count + seq, parts * own_rows :, :].astype(F32)
        odd = block_ref[(m + 1) * seq_count + seq, parts * own_rows :, :].astype(F32)
        first = row < own_rows // 2
        both = jnp.where(first, even, odd)
        bias.append(jnp.where(first != lower, both, pltpu.roll(both, cells, 1)))
    bias = jnp.concatenate(bias, axis=0)
    wide = iota((residues, LANES), 1) < cells

    attended = []
    for m in range(0, members, 2):
        keys = key_values[m * residues : (m + 2) * residues, :inner]
        values = key_values[m * residues : (m + 2) * residues, inner:]
        scores = lax.dot_general(
            keys, spread[m * cells : (m + 2) * cells], (((1,), (1,)), ((), ())),
            preferred_element_type=F32,
        )
        scores = jnp.where(wide, scores[:residues], scores[residues:]) * scaling + bias
        keep = jnp.concatenate(
            [jnp.where(lower, tails[m][s], tails[m + 1][s]) for s in range(seq_count)], axis=0
        )
        scores = jnp.where(keep > 0, scores, -1000000000.0)
        scores = jnp.exp(scores - jnp.max(scores, axis=0, keepdims=True))
        weights = scores / jnp.sum(scores, axis=0, keepdims=True)
        weights = jnp.concatenate(
            [jnp.where(wide, weights, 0.0), jnp.where(wide, 0.0, weights)], axis=0
        ).astype(BF16)
        mixed = lax.dot_general(
            weights, values, (((0,), (0,)), ((), ())), preferred_element_type=F32
        )
        mixed = mixed.reshape(2, heads, own_rows, inner) * head_of[None]
        attended.append(jnp.sum(mixed, axis=1))
    attended = jnp.concatenate(attended, axis=0).reshape(tokens, inner)
    gated = (jax.nn.sigmoid(gates) * attended).astype(BF16)
    residual = jnp.concatenate(
        [
            jnp.concatenate([part(m * seq_count + seq, k) for k in range(parts)], axis=1)
            for m in range(members)
        ],
        axis=0,
    )
    one = (residual + mm(gated, row_out_ref[...])).astype(BF16).astype(F32)
    one_ref[...] = one.reshape(members, own_rows, width)

    second = normalize_rows(one)
    second_ref[...] = second.reshape(members, own_rows, width)
    key_values = mm(second, column_proj_ref[:, inner : 3 * inner]).astype(BF16).astype(F32)
    own = second_ref[dap]
    queries = mm(own, column_proj_ref[:, :inner]).astype(BF16).astype(F32)
    gates = mm(own, column_proj_ref[:, 3 * inner :]).astype(BF16).astype(F32)
    products = (
        key_values[:, :inner].reshape(members, own_rows, inner) * queries[None]
    ).reshape(tokens, inner)
    high = products.astype(BF16)
    low = (products - high.astype(F32)).astype(BF16)
    same_head = (iota((inner, inner), 0) // depth == iota((inner, inner), 1) // depth).astype(
        F32
    ).astype(BF16)
    scores = (mm(high, same_head) + mm(low, same_head)) * scaling
    scores = scores.reshape(members, own_rows, inner)
    keep = []
    for m in range(members):
        tail = block_ref[m * seq_count + seq, parts * own_rows :, :].astype(F32)
        mine = lower if m % 2 == 0 else jnp.logical_not(lower)
        tail = jnp.where(mine, tail, pltpu.roll(tail, cells, 1))
        keep.append(jnp.concatenate([tail] * (inner // LANES), axis=1)[None])
    keep = jnp.concatenate(keep, axis=0)
    scores = jnp.where(keep > 0, scores, -1000000000.0)
    scores = jnp.exp(scores - jnp.max(scores, axis=0, keepdims=True))
    weights = (scores / jnp.sum(scores, axis=0, keepdims=True)).astype(BF16).astype(F32)
    attended = jnp.sum(
        weights * key_values[:, inner:].reshape(members, own_rows, inner), axis=0
    )
    gated = (jax.nn.sigmoid(gates) * attended).astype(BF16)
    two = one_ref[dap] + mm(gated, column_out_ref[...])
    hidden = jnp.maximum(mm(normalize_rows(two), expansion_ref[...]), 0.0).astype(BF16)
    out_ref[0] = (two + mm(hidden, contraction_ref[...])).astype(BF16)


def whole_body(
    homolog_tensor,
    pair_features,
    entry_real_mask,
    chain_ids,
    horizontal_matrices,
    horizontal_projector,
    bias_proj,
    chain_bias,
    column_proj,
    vertical_projector,
    expansion_matrix,
    contraction_matrix,
):
    _, own_rows, width = homolog_tensor.shape
    dap_count, seq_count = lax.axis_size("dap"), lax.axis_size("seq")
    count = dap_count * seq_count
    rows = own_rows * (width // LANES + 1)
    vmem, smem = (pl.BlockSpec(memory_space=space) for space in (pltpu.VMEM, pltpu.SMEM))
    packed = pl.pallas_call(
        pack_kernel,
        out_shape=jax.ShapeDtypeStruct((count, rows, LANES), BF16),
        in_specs=[vmem, vmem, smem, vmem, smem, smem],
        out_specs=vmem,
        compiler_params=pltpu.CompilerParams(vmem_limit_bytes=8 << 20),
    )(homolog_tensor, pair_features, entry_real_mask, bias_proj, chain_ids, chain_bias)
    blocks = lax.all_to_all(packed, ("dap", "seq"), split_axis=0, concat_axis=0, tiled=True)
    return pl.pallas_call(
        lambda *refs: block_kernel(seq_count, *refs),
        out_shape=jax.ShapeDtypeStruct(homolog_tensor.shape, BF16),
        in_specs=[vmem] * 7,
        out_specs=vmem,
        scratch_shapes=[
            pltpu.VMEM((dap_count, seq_count, own_rows, width), BF16),
            pltpu.VMEM((dap_count, own_rows, width), BF16),
            pltpu.VMEM((dap_count, own_rows, width), F32),
        ],
        compiler_params=pltpu.CompilerParams(vmem_limit_bytes=16 << 20),
    )(
        blocks,
        horizontal_matrices,
        horizontal_projector,
        column_proj,
        vertical_projector,
        expansion_matrix,
        contraction_matrix,
    )


def fits_whole(homolog_tensor, pair_features, dap_count):
    row_count, local_residues, width = homolog_tensor.shape
    queries, keys, pair_width = pair_features.shape
    return (
        row_count == 1
        and local_residues == SUBLANES
        and queries == local_residues
        and 2 * keys == SUBLANES
        and dap_count % 2 == 0
        and 2 * HEAD_TOTAL * queries == LANES
        and width % LANES == 0
        and pair_width == LANES
        and HEAD_TOTAL * HEAD_DEPTH % LANES == 0
        and lax.axis_size("seq") * dap_count * homolog_tensor.size * 2 <= WHOLE_BYTES
    )


def choose(*operands):
    whole = fits_whole(operands[0], operands[1], lax.axis_size("dap"))
    return whole_body(*operands) if whole else body(*operands)


def solution(mesh):
    placed = (
        P("dap", "seq", None),
        P("seq", "dap", None),
        P("dap", "seq"),
        P(),
        P(),
        P(),
        P(),
        P(),
        P(),
        P(),
        P(),
        P(),
    )
    return jax.shard_map(
        choose, mesh=mesh, in_specs=placed, out_specs=P("dap", "seq", None), check_vma=False
    )
```

```python
import jax
import jax.numpy as jnp
from jax import lax
from jax.experimental import pallas as pl
from jax.experimental.pallas import tpu as pltpu
from jax.sharding import PartitionSpec as P

HEAD_TOTAL = 8
HEAD_DEPTH = 32


epsilon = 1e-05


def layer_norm(inputs):
    center = inputs - jnp.mean(inputs, axis=-1, keepdims=True)
    spread = jnp.mean(center * center, axis=-1, keepdims=True)
    return center * lax.rsqrt(spread + epsilon)


def attend(queries, key_part, value_part, keep_mask, bias_term):
    scores = jnp.einsum(
        "ihd,jhd->hij", queries, key_part, preferred_element_type=jnp.float32
    ) * HEAD_DEPTH ** (-0.5)
    if bias_term is not None:
        scores = scores + bias_term.astype(jnp.float32)
    scores = jnp.where(keep_mask[None, None, :] > 0, scores, -1000000000.0)
    weights = jax.nn.softmax(scores, axis=-1).astype(jnp.bfloat16)
    return jnp.einsum("hij,jhd->ihd", weights, value_part, preferred_element_type=jnp.float32)


def column_update(
    column, keep_column, column_proj, vertical_projector, expansion_matrix, contraction_matrix
):
    expanded_dimension = HEAD_TOTAL * HEAD_DEPTH
    standardized = layer_norm(column.astype(jnp.float32)).astype(jnp.bfloat16)
    projected = jnp.dot(standardized, column_proj, preferred_element_type=jnp.float32).astype(
        jnp.bfloat16
    )
    queries = projected[:, :expanded_dimension].reshape(-1, HEAD_TOTAL, HEAD_DEPTH)
    key_part = projected[:, expanded_dimension : 2 * expanded_dimension].reshape(
        -1, HEAD_TOTAL, HEAD_DEPTH
    )
    value_part = projected[:, 2 * expanded_dimension : 3 * expanded_dimension].reshape(
        -1, HEAD_TOTAL, HEAD_DEPTH
    )
    attended = attend(queries, key_part, value_part, keep_column, None).reshape(
        -1, expanded_dimension
    )
    sigmoid_scaled = (
        jax.nn.sigmoid(projected[:, 3 * expanded_dimension :].astype(jnp.float32)) * attended
    ).astype(jnp.bfloat16)
    mixed = column.astype(jnp.float32) + jnp.dot(
        sigmoid_scaled, vertical_projector, preferred_element_type=jnp.float32
    )
    inner = jnp.maximum(
        jnp.dot(
            layer_norm(mixed).astype(jnp.bfloat16),
            expansion_matrix,
            preferred_element_type=jnp.float32,
        ),
        0.0,
    ).astype(jnp.bfloat16)
    return (mixed + jnp.dot(inner, contraction_matrix, preferred_element_type=jnp.float32)).astype(
        jnp.bfloat16
    )


def body(
    homolog_tensor,
    pair_features,
    entry_real_mask,
    chain_ids,
    horizontal_matrices,
    horizontal_projector,
    bias_proj,
    chain_bias,
    column_proj,
    vertical_projector,
    expansion_matrix,
    contraction_matrix,
):
    row_count, local_residues, channels = homolog_tensor.shape
    expanded_dimension = HEAD_TOTAL * HEAD_DEPTH
    dap_count = lax.axis_size("dap")
    pair_rows, pair_columns, pair_width = pair_features.shape
    normed_pair = layer_norm(pair_features.astype(jnp.float32))
    projected_pair = jnp.einsum(
        "ijc,ch->hij", normed_pair, bias_proj, precision=lax.Precision.HIGHEST
    )
    row_chain = lax.dynamic_slice_in_dim(chain_ids, lax.axis_index("seq") * pair_rows, pair_rows)
    column_chain = lax.dynamic_slice_in_dim(
        chain_ids, lax.axis_index("dap") * pair_columns, pair_columns
    )
    same_chain = (row_chain[:, None] == column_chain[None, :]).astype(jnp.float32)
    chain_term = chain_bias[0][:, None, None] * same_chain + chain_bias[1][:, None, None] * (
        1.0 - same_chain
    )
    local_bias = (projected_pair + chain_term).astype(jnp.bfloat16)
    pair_bias = lax.all_gather(local_bias, "dap", axis=2, tiled=True)
    standardized = layer_norm(homolog_tensor.astype(jnp.float32)).astype(jnp.bfloat16)
    flat = standardized.reshape(-1, channels)
    keep_mask = entry_real_mask.astype(jnp.bfloat16)
    projected = (
        jnp.dot(flat, horizontal_matrices, preferred_element_type=jnp.float32)
        .astype(jnp.bfloat16)
        .reshape(row_count, local_residues, 4 * expanded_dimension)
    )
    queries = projected[..., :expanded_dimension]
    gating = projected[..., 3 * expanded_dimension :]
    key_values, keep_all = (
        lax.all_gather(
            projected[..., expanded_dimension : 3 * expanded_dimension], "seq", axis=1, tiled=True
        ),
        lax.all_gather(keep_mask, "seq", axis=1, tiled=True),
    )

    def one_row(inputs_row):
        row_queries, row_pairs, row_keep = inputs_row
        key_part = row_pairs[:, :expanded_dimension].reshape(-1, HEAD_TOTAL, HEAD_DEPTH)
        value_part = row_pairs[:, expanded_dimension:].reshape(-1, HEAD_TOTAL, HEAD_DEPTH)
        return attend(
            row_queries.reshape(local_residues, HEAD_TOTAL, HEAD_DEPTH),
            key_part,
            value_part,
            row_keep,
            pair_bias,
        ).reshape(local_residues, expanded_dimension)

    attended = lax.map(one_row, (queries, key_values, keep_all))
    sigmoid_scaled = (jax.nn.sigmoid(gating.astype(jnp.float32)) * attended).astype(jnp.bfloat16)
    row_result = jnp.dot(
        sigmoid_scaled.reshape(-1, expanded_dimension),
        horizontal_projector,
        preferred_element_type=jnp.float32,
    ).reshape(row_count, local_residues, channels)
    updated_rows = (homolog_tensor.astype(jnp.float32) + row_result).astype(jnp.bfloat16)
    per_device = local_residues // dap_count
    blocks = updated_rows.reshape(row_count, dap_count, per_device, channels)
    keep_blocks = keep_mask.reshape(row_count, dap_count, per_device)

    def single_column(inputs_col):
        return column_update(
            inputs_col[0],
            inputs_col[1],
            column_proj,
            vertical_projector,
            expansion_matrix,
            contraction_matrix,
        )

    column_block = lax.all_to_all(blocks, "dap", split_axis=1, concat_axis=0, tiled=True)
    column_keep = lax.all_to_all(keep_blocks, "dap", split_axis=1, concat_axis=0, tiled=True)
    inputs_col = (jnp.moveaxis(column_block[:, 0], 1, 0), jnp.moveaxis(column_keep[:, 0], 1, 0))
    output_list = lax.map(single_column, inputs_col)
    mixed = jnp.moveaxis(output_list, 0, 1)[:, None]
    returned = lax.all_to_all(mixed, "dap", split_axis=0, concat_axis=1, tiled=True)
    return returned.reshape(row_count, local_residues, channels)


LANES = 128
SUBLANES = 8
WHOLE_BYTES = 1 << 20
F32 = jnp.float32
BF16 = jnp.bfloat16


def mm(a, b):
    return lax.dot_general(a, b, (((1,), (0,)), ((), ())), preferred_element_type=F32)


def iota(shape, axis):
    return lax.broadcasted_iota(jnp.int32, shape, axis)


def normalize(parts, width):
    total = parts[0]
    for part in parts[1:]:
        total = total + part
    mean = jnp.sum(total, axis=-1, keepdims=True) * (1.0 / width)
    center = [part - mean for part in parts]
    total = center[0] * center[0]
    for part in center[1:]:
        total = total + part * part
    scale = lax.rsqrt(jnp.sum(total, axis=-1, keepdims=True) * (1.0 / width) + epsilon)
    return [part * scale for part in center]


def halves(x):
    return [x[:, k : k + LANES] for k in range(0, x.shape[1], LANES)]


def normalize_rows(x):
    return jnp.concatenate(normalize(halves(x), x.shape[1]), axis=1).astype(BF16)


def pack_kernel(*refs):
    count = (len(refs) - 2) // 2
    out_ref, arrived = refs[count], refs[-1]
    near = refs[count + 1 : -1]
    copies = [
        pltpu.make_async_copy(source, target, arrived.at[k])
        for k, (source, target) in enumerate(zip(refs[:count], near))
    ]
    for copy in copies:
        copy.start()
    for copy in copies:
        copy.wait()
    pair_ref, proj_ref, msa_ref, chain_ref, chain_bias_ref, mask_ref = near
    queries, keys, width = pair_ref.shape
    cells = HEAD_TOTAL * queries
    dap, seq = lax.axis_index("dap"), lax.axis_index("seq")
    odd = lax.rem(dap, 2)
    pairs = queries * keys
    normed = normalize([pair_ref[...].astype(F32).reshape(pairs, width)], width)[0]
    bias = lax.dot_general(
        proj_ref[...], normed, (((1,), (1,)), ((), ())),
        precision=lax.Precision.HIGHEST, preferred_element_type=F32,
    )
    shape = bias.shape
    head, pair = iota(shape, 0), iota(shape, 1)
    key_chain, query_chain = jnp.zeros(shape, jnp.int32), jnp.zeros(shape, jnp.int32)
    for k in range(keys):
        key_chain = jnp.where(pair % keys == k, chain_ref[dap * keys + k], key_chain)
    for k in range(queries):
        query_chain = jnp.where(pair // keys == k, chain_ref[seq * queries + k], query_chain)
    same, other = jnp.zeros(shape, F32), jnp.zeros(shape, F32)
    for h in range(HEAD_TOTAL):
        same = jnp.where(head == h, chain_bias_ref[0, h], same)
        other = jnp.where(head == h, chain_bias_ref[1, h], other)
    bias = (bias + jnp.where(key_chain == query_chain, same, other)).astype(BF16)
    heads = (iota((HEAD_TOTAL, LANES), 1) % cells // queries == iota((HEAD_TOTAL, LANES), 0)).astype(F32)
    bias = lax.dot_general(
        bias, heads.astype(BF16), (((0,), (0,)), ((), ())), preferred_element_type=F32
    )
    own = iota(bias.shape, 1) % queries == iota(bias.shape, 0) // keys
    bias = jnp.where(own, bias, 0.0).reshape(pairs // SUBLANES, SUBLANES, LANES)
    bias = jnp.sum(bias, axis=0)
    bias = bias + pltpu.roll(bias, keys, 0)
    shape = bias.shape
    row, lane = iota(shape, 0), iota(shape, 1)
    mask = jnp.zeros(shape, F32)
    for k in range(SUBLANES):
        mask = jnp.where(row == k, mask_ref[0, k].astype(F32), mask)
    upper = (lane >= cells).astype(jnp.int32)
    tail = jnp.where(upper != odd, bias, mask)
    block = jnp.concatenate([*halves(msa_ref[0].astype(F32)), tail], axis=0).astype(BF16)
    out_ref[...] = jnp.broadcast_to(block[None], out_ref.shape)


def block_kernel(
    seq_count, block_ref, row_proj_ref, row_out_far, column_proj_far, column_out_far, expansion_far,
    contraction_far, out_ref, second_ref, one_ref, row_out_ref, column_proj_ref,
    column_out_ref, expansion_ref, contraction_ref, arrived, fence,
):
    far = (row_out_far, column_proj_far, column_out_far, expansion_far, contraction_far)
    near = (row_out_ref, column_proj_ref, column_out_ref, expansion_ref, contraction_ref)
    copies = [
        pltpu.make_async_copy(source, target, arrived.at[k])
        for k, (source, target) in enumerate(zip(far, near))
    ]
    for copy in copies:
        copy.start()
    pl.semaphore_signal(fence, 1)
    pl.semaphore_wait(fence, 1)
    count, rows, _ = block_ref.shape
    own_rows = SUBLANES
    width = rows * LANES // own_rows - LANES
    parts = width // LANES
    members = count // seq_count
    residues = seq_count * own_rows
    heads, depth = HEAD_TOTAL, HEAD_DEPTH
    inner = heads * depth
    cells = heads * own_rows
    tokens = members * own_rows
    dap, seq = lax.axis_index("dap"), lax.axis_index("seq")
    scaling = depth**-0.5

    def part(ref_index, k):
        return block_ref[ref_index, k * own_rows : (k + 1) * own_rows, :].astype(F32)

    def tail(m, s):
        return block_ref[m * seq_count + s, parts * own_rows :, :].astype(F32)

    def mine(k):
        return jnp.concatenate([part(m * seq_count + seq, k) for m in range(members)], axis=0)

    residual = [mine(k) for k in range(parts)]
    own = jnp.concatenate(normalize(residual, width), axis=1).astype(BF16)
    queries = mm(own, row_proj_ref[:, :inner]).astype(BF16).astype(F32)
    gates = mm(own, row_proj_ref[:, 3 * inner :]).astype(BF16).astype(F32)
    everything = slice(None)
    x = [part(everything, k).reshape(count * own_rows, LANES) for k in range(parts)]
    normed = jnp.concatenate(normalize(x, width), axis=1).astype(BF16)
    all_keys = mm(normed, row_proj_ref[:, inner : 2 * inner]).astype(BF16)
    all_values = mm(normed, row_proj_ref[:, 2 * inner : 3 * inner]).astype(BF16)

    head_of = iota((heads, 1, inner), 2) // depth == iota((heads, 1, inner), 0)
    spread = jnp.where(
        head_of[None], queries.reshape(members, 1, own_rows, inner), 0.0
    ).reshape(members * cells, inner).astype(BF16)

    shape = (own_rows, LANES)
    row, lane = iota(shape, 0), iota(shape, 1)
    lower = lane < cells
    bias = []
    for m in range(0, members, 2):
        first = row < own_rows // 2
        both = jnp.where(first, tail(m, seq), tail(m + 1, seq))
        bias.append(jnp.where(first != lower, both, pltpu.roll(both, cells, 1)))
    bias = jnp.concatenate(bias, axis=0)
    wide = iota((residues, LANES), 1) < cells
    keeps = [
        jnp.concatenate(
            [jnp.where(lower, tail(m, s), tail(m + 1, s)) for s in range(seq_count)], axis=0
        ) > 0
        for m in range(0, members, 2)
    ]

    scores = [
        lax.dot_general(
            all_keys[m * residues : (m + 2) * residues],
            spread[m * cells : (m + 2) * cells],
            (((1,), (1,)), ((), ())),
            preferred_element_type=F32,
        )
        for m in range(0, members, 2)
    ]
    scores = [jnp.where(wide, two[:residues], two[residues:]) * scaling + bias for two in scores]
    scores = [jnp.where(keep, two, -1000000000.0) for two, keep in zip(scores, keeps)]
    scores = [jnp.exp(two - jnp.max(two, axis=0, keepdims=True)) for two in scores]
    weights = [two / jnp.sum(two, axis=0, keepdims=True) for two in scores]
    weights = [
        jnp.concatenate([jnp.where(wide, two, 0.0), jnp.where(wide, 0.0, two)], axis=0).astype(BF16)
        for two in weights
    ]
    mixed = [
        lax.dot_general(
            two, all_values[2 * k * residues : 2 * (k + 1) * residues],
            (((0,), (0,)), ((), ())), preferred_element_type=F32,
        )
        for k, two in enumerate(weights)
    ]
    mixed = [
        jnp.sum(jnp.where(head_of[None], two.reshape(2, heads, own_rows, inner), 0.0), axis=1)
        for two in mixed
    ]
    attended = jnp.concatenate(mixed, axis=0).reshape(tokens, inner)
    gated = (jax.nn.sigmoid(gates) * attended).astype(BF16)
    copies[0].wait()
    one = (jnp.concatenate(residual, axis=1) + mm(gated, row_out_ref[...])).astype(BF16).astype(F32)
    one_ref[...] = one.reshape(members, own_rows, width)

    second = normalize_rows(one)
    second_ref[...] = second.reshape(members, own_rows, width)
    copies[1].wait()
    key_values = mm(second, column_proj_ref[:, inner : 3 * inner]).astype(BF16).astype(F32)
    own = second_ref[dap]
    queries = mm(own, column_proj_ref[:, :inner]).astype(BF16).astype(F32)
    gates = mm(own, column_proj_ref[:, 3 * inner :]).astype(BF16).astype(F32)
    products = (
        key_values[:, :inner].reshape(members, own_rows, inner) * queries[None]
    ).reshape(tokens, inner)
    high = products.astype(BF16)
    low = (products - high.astype(F32)).astype(BF16)
    same_head = (iota((inner, inner), 0) // depth == iota((inner, inner), 1) // depth).astype(
        F32
    ).astype(BF16)
    scores = (mm(high, same_head) + mm(low, same_head)) * scaling
    scores = scores.reshape(members, own_rows, inner)
    keep = []
    for m in range(members):
        mask = tail(m, seq)
        valid = lower if m % 2 == 0 else jnp.logical_not(lower)
        mask = jnp.where(valid, mask, pltpu.roll(mask, cells, 1))
        keep.append(jnp.concatenate([mask] * (inner // LANES), axis=1)[None])
    keep = jnp.concatenate(keep, axis=0)
    scores = jnp.where(keep > 0, scores, -1000000000.0)
    scores = jnp.exp(scores - jnp.max(scores, axis=0, keepdims=True))
    weights = (scores / jnp.sum(scores, axis=0, keepdims=True)).astype(BF16).astype(F32)
    attended = jnp.sum(
        weights * key_values[:, inner:].reshape(members, own_rows, inner), axis=0
    )
    gated = (jax.nn.sigmoid(gates) * attended).astype(BF16)
    copies[2].wait()
    two = one_ref[dap] + mm(gated, column_out_ref[...])
    copies[3].wait()
    hidden = jnp.maximum(mm(normalize_rows(two), expansion_ref[...]), 0.0).astype(BF16)
    copies[4].wait()
    out_ref[0] = (two + mm(hidden, contraction_ref[...])).astype(BF16)


def whole_body(
    homolog_tensor,
    pair_features,
    entry_real_mask,
    chain_ids,
    horizontal_matrices,
    horizontal_projector,
    bias_proj,
    chain_bias,
    column_proj,
    vertical_projector,
    expansion_matrix,
    contraction_matrix,
):
    _, own_rows, width = homolog_tensor.shape
    dap_count, seq_count = lax.axis_size("dap"), lax.axis_size("seq")
    count = dap_count * seq_count
    rows = own_rows * (width // LANES + 1)
    vmem, hbm = (pl.BlockSpec(memory_space=space) for space in (pltpu.VMEM, pltpu.HBM))
    vectors = [pair_features, bias_proj.T, homolog_tensor]
    scalars = [chain_ids, chain_bias, entry_real_mask]
    packed = pl.pallas_call(
        pack_kernel,
        out_shape=jax.ShapeDtypeStruct((count, rows, LANES), BF16),
        in_specs=[hbm] * len(vectors + scalars),
        out_specs=vmem,
        scratch_shapes=[
            *(pltpu.VMEM(operand.shape, operand.dtype) for operand in vectors),
            *(pltpu.SMEM(operand.shape, operand.dtype) for operand in scalars),
            pltpu.SemaphoreType.DMA((len(vectors + scalars),)),
        ],
        compiler_params=pltpu.CompilerParams(vmem_limit_bytes=8 << 20),
    )(*map(in_hbm, vectors + scalars))
    blocks = lax.all_to_all(packed, ("dap", "seq"), split_axis=0, concat_axis=0, tiled=True)
    later = [
        horizontal_projector, column_proj, vertical_projector, expansion_matrix, contraction_matrix
    ]
    return pl.pallas_call(
        lambda *refs: block_kernel(seq_count, *refs),
        out_shape=jax.ShapeDtypeStruct(homolog_tensor.shape, BF16),
        in_specs=[vmem] * 2 + [hbm] * len(later),
        out_specs=vmem,
        scratch_shapes=[
            pltpu.VMEM((dap_count, own_rows, width), BF16),
            pltpu.VMEM((dap_count, own_rows, width), F32),
            *(pltpu.VMEM(weight.shape, weight.dtype) for weight in later),
            pltpu.SemaphoreType.DMA((len(later),)),
            pltpu.SemaphoreType.REGULAR,
        ],
        compiler_params=pltpu.CompilerParams(vmem_limit_bytes=16 << 20),
    )(blocks, horizontal_matrices, *map(in_hbm, later))


def in_hbm(operand):
    return pltpu.with_memory_space_constraint(operand, pltpu.HBM)


def fits_whole(homolog_tensor, pair_features, dap_count):
    row_count, local_residues, width = homolog_tensor.shape
    queries, keys, pair_width = pair_features.shape
    return (
        row_count == 1
        and local_residues == SUBLANES
        and queries == local_residues
        and 2 * keys == SUBLANES
        and dap_count % 2 == 0
        and 2 * HEAD_TOTAL * queries == LANES
        and width % LANES == 0
        and pair_width == LANES
        and HEAD_TOTAL * HEAD_DEPTH % LANES == 0
        and lax.axis_size("seq") * dap_count * homolog_tensor.size * 2 <= WHOLE_BYTES
    )


def choose(*operands):
    whole = fits_whole(operands[0], operands[1], lax.axis_size("dap"))
    return whole_body(*operands) if whole else body(*operands)


def solution(mesh):
    placed = (
        P("dap", "seq", None),
        P("seq", "dap", None),
        P("dap", "seq"),
        P(),
        P(),
        P(),
        P(),
        P(),
        P(),
        P(),
        P(),
        P(),
    )
    return jax.shard_map(
        choose, mesh=mesh, in_specs=placed, out_specs=P("dap", "seq", None), check_vma=False
    )
```

```python
import jax
import jax.numpy as jnp
from jax import lax
from jax.experimental import pallas as pl
from jax.experimental.pallas import tpu as pltpu
from jax.sharding import Mesh, PartitionSpec as P

HEAD_TOTAL = 8
HEAD_DEPTH = 32


epsilon = 1e-05


def layer_norm(inputs):
    center = inputs - jnp.mean(inputs, axis=-1, keepdims=True)
    spread = jnp.mean(center * center, axis=-1, keepdims=True)
    return center * lax.rsqrt(spread + epsilon)


def attend(queries, key_part, value_part, keep_mask, bias_term):
    scores = jnp.einsum(
        "ihd,jhd->hij", queries, key_part, preferred_element_type=jnp.float32
    ) * HEAD_DEPTH ** (-0.5)
    if bias_term is not None:
        scores = scores + bias_term.astype(jnp.float32)
    scores = jnp.where(keep_mask[None, None, :] > 0, scores, -1000000000.0)
    weights = jax.nn.softmax(scores, axis=-1).astype(jnp.bfloat16)
    return jnp.einsum("hij,jhd->ihd", weights, value_part, preferred_element_type=jnp.float32)


def column_update(
    column, keep_column, column_proj, vertical_projector, expansion_matrix, contraction_matrix
):
    expanded_dimension = HEAD_TOTAL * HEAD_DEPTH
    standardized = layer_norm(column.astype(jnp.float32)).astype(jnp.bfloat16)
    projected = jnp.dot(standardized, column_proj, preferred_element_type=jnp.float32).astype(
        jnp.bfloat16
    )
    queries = projected[:, :expanded_dimension].reshape(-1, HEAD_TOTAL, HEAD_DEPTH)
    key_part = projected[:, expanded_dimension : 2 * expanded_dimension].reshape(
        -1, HEAD_TOTAL, HEAD_DEPTH
    )
    value_part = projected[:, 2 * expanded_dimension : 3 * expanded_dimension].reshape(
        -1, HEAD_TOTAL, HEAD_DEPTH
    )
    attended = attend(queries, key_part, value_part, keep_column, None).reshape(
        -1, expanded_dimension
    )
    sigmoid_scaled = (
        jax.nn.sigmoid(projected[:, 3 * expanded_dimension :].astype(jnp.float32)) * attended
    ).astype(jnp.bfloat16)
    mixed = column.astype(jnp.float32) + jnp.dot(
        sigmoid_scaled, vertical_projector, preferred_element_type=jnp.float32
    )
    inner = jnp.maximum(
        jnp.dot(
            layer_norm(mixed).astype(jnp.bfloat16),
            expansion_matrix,
            preferred_element_type=jnp.float32,
        ),
        0.0,
    ).astype(jnp.bfloat16)
    return (mixed + jnp.dot(inner, contraction_matrix, preferred_element_type=jnp.float32)).astype(
        jnp.bfloat16
    )


def body(
    homolog_tensor,
    pair_features,
    entry_real_mask,
    chain_ids,
    horizontal_matrices,
    horizontal_projector,
    bias_proj,
    chain_bias,
    column_proj,
    vertical_projector,
    expansion_matrix,
    contraction_matrix,
):
    row_count, local_residues, channels = homolog_tensor.shape
    expanded_dimension = HEAD_TOTAL * HEAD_DEPTH
    dap_count = lax.axis_size("dap")
    pair_rows, pair_columns, pair_width = pair_features.shape
    normed_pair = layer_norm(pair_features.astype(jnp.float32))
    projected_pair = jnp.einsum(
        "ijc,ch->hij", normed_pair, bias_proj, precision=lax.Precision.HIGHEST
    )
    row_chain = lax.dynamic_slice_in_dim(chain_ids, lax.axis_index("seq") * pair_rows, pair_rows)
    column_chain = lax.dynamic_slice_in_dim(
        chain_ids, lax.axis_index("dap") * pair_columns, pair_columns
    )
    same_chain = (row_chain[:, None] == column_chain[None, :]).astype(jnp.float32)
    chain_term = chain_bias[0][:, None, None] * same_chain + chain_bias[1][:, None, None] * (
        1.0 - same_chain
    )
    local_bias = (projected_pair + chain_term).astype(jnp.bfloat16)
    pair_bias = lax.all_gather(local_bias, "dap", axis=2, tiled=True)
    standardized = layer_norm(homolog_tensor.astype(jnp.float32)).astype(jnp.bfloat16)
    flat = standardized.reshape(-1, channels)
    keep_mask = entry_real_mask.astype(jnp.bfloat16)
    projected = (
        jnp.dot(flat, horizontal_matrices, preferred_element_type=jnp.float32)
        .astype(jnp.bfloat16)
        .reshape(row_count, local_residues, 4 * expanded_dimension)
    )
    queries = projected[..., :expanded_dimension]
    gating = projected[..., 3 * expanded_dimension :]
    key_values, keep_all = (
        lax.all_gather(
            projected[..., expanded_dimension : 3 * expanded_dimension], "seq", axis=1, tiled=True
        ),
        lax.all_gather(keep_mask, "seq", axis=1, tiled=True),
    )

    def one_row(inputs_row):
        row_queries, row_pairs, row_keep = inputs_row
        key_part = row_pairs[:, :expanded_dimension].reshape(-1, HEAD_TOTAL, HEAD_DEPTH)
        value_part = row_pairs[:, expanded_dimension:].reshape(-1, HEAD_TOTAL, HEAD_DEPTH)
        return attend(
            row_queries.reshape(local_residues, HEAD_TOTAL, HEAD_DEPTH),
            key_part,
            value_part,
            row_keep,
            pair_bias,
        ).reshape(local_residues, expanded_dimension)

    attended = lax.map(one_row, (queries, key_values, keep_all))
    sigmoid_scaled = (jax.nn.sigmoid(gating.astype(jnp.float32)) * attended).astype(jnp.bfloat16)
    row_result = jnp.dot(
        sigmoid_scaled.reshape(-1, expanded_dimension),
        horizontal_projector,
        preferred_element_type=jnp.float32,
    ).reshape(row_count, local_residues, channels)
    updated_rows = (homolog_tensor.astype(jnp.float32) + row_result).astype(jnp.bfloat16)
    per_device = local_residues // dap_count
    blocks = updated_rows.reshape(row_count, dap_count, per_device, channels)
    keep_blocks = keep_mask.reshape(row_count, dap_count, per_device)

    def single_column(inputs_col):
        return column_update(
            inputs_col[0],
            inputs_col[1],
            column_proj,
            vertical_projector,
            expansion_matrix,
            contraction_matrix,
        )

    column_block = lax.all_to_all(blocks, "dap", split_axis=1, concat_axis=0, tiled=True)
    column_keep = lax.all_to_all(keep_blocks, "dap", split_axis=1, concat_axis=0, tiled=True)
    inputs_col = (jnp.moveaxis(column_block[:, 0], 1, 0), jnp.moveaxis(column_keep[:, 0], 1, 0))
    output_list = lax.map(single_column, inputs_col)
    mixed = jnp.moveaxis(output_list, 0, 1)[:, None]
    returned = lax.all_to_all(mixed, "dap", split_axis=0, concat_axis=1, tiled=True)
    return returned.reshape(row_count, local_residues, channels)


LANES = 128
SUBLANES = 8
WHOLE_BYTES = 1 << 20
F32 = jnp.float32
BF16 = jnp.bfloat16


def mm(a, b):
    return lax.dot_general(a, b, (((1,), (0,)), ((), ())), preferred_element_type=F32)


def iota(shape, axis):
    return lax.broadcasted_iota(jnp.int32, shape, axis)


def normalize(parts, width):
    total = parts[0]
    for part in parts[1:]:
        total = total + part
    mean = jnp.sum(total, axis=-1, keepdims=True) * (1.0 / width)
    center = [part - mean for part in parts]
    total = center[0] * center[0]
    for part in center[1:]:
        total = total + part * part
    scale = lax.rsqrt(jnp.sum(total, axis=-1, keepdims=True) * (1.0 / width) + epsilon)
    return [part * scale for part in center]


def halves(x):
    return [x[:, k : k + LANES] for k in range(0, x.shape[1], LANES)]


def normalize_rows(x):
    return jnp.concatenate(normalize(halves(x), x.shape[1]), axis=1).astype(BF16)


def pack_kernel(*refs):
    count = (len(refs) - 2) // 2
    out_ref, arrived = refs[count], refs[-1]
    near = refs[count + 1 : -1]
    copies = [
        pltpu.make_async_copy(source, target, arrived.at[k])
        for k, (source, target) in enumerate(zip(refs[:count], near))
    ]
    for copy in copies:
        copy.start()
    for copy in copies:
        copy.wait()
    pair_ref, proj_ref, msa_ref, chain_ref, chain_bias_ref, mask_ref = near
    queries, keys, width = pair_ref.shape
    cells = HEAD_TOTAL * queries
    far, seq = lax.axis_index("far"), lax.axis_index("seq")
    dap = far * lax.axis_size("near") + lax.axis_index("near")
    pairs = queries * keys

    block = jnp.concatenate(halves(msa_ref[0].astype(F32)), axis=0).astype(BF16)
    out_ref[:, : block.shape[0], :] = jnp.broadcast_to(block[None], (out_ref.shape[0], *block.shape))

    pair = pair_ref[...].astype(F32).reshape(pairs, width)
    center = pair - jnp.sum(pair, axis=-1, keepdims=True) * (1.0 / width)
    spread = jnp.sum(center * center, axis=-1, keepdims=True) * (1.0 / width)
    shape = (pairs, LANES)
    lane = iota(shape, 1)
    bias = jnp.zeros(shape, F32)
    for h in range(HEAD_TOTAL):
        projected = jnp.sum(center * proj_ref[h : h + 1, :], axis=-1, keepdims=True)
        bias = jnp.where(lane % cells // queries == h, projected, bias)
    bias = bias * lax.rsqrt(spread + epsilon)
    bias = jnp.where(lane % queries == iota(shape, 0) // keys, bias, 0.0)
    bias = jnp.sum(bias.reshape(pairs // SUBLANES, SUBLANES, LANES), axis=0)
    bias = bias + pltpu.roll(bias, keys, 0)

    shape = bias.shape
    row, lane = iota(shape, 0), iota(shape, 1)
    key_chain, query_chain = jnp.zeros(shape, jnp.int32), jnp.zeros(shape, jnp.int32)
    for k in range(keys):
        key_chain = jnp.where(row % keys == k, chain_ref[dap * keys + k], key_chain)
    for k in range(queries):
        query_chain = jnp.where(lane % queries == k, chain_ref[seq * queries + k], query_chain)
    same, other = jnp.zeros(shape, F32), jnp.zeros(shape, F32)
    for h in range(HEAD_TOTAL):
        here = lane % cells // queries == h
        same = jnp.where(here, chain_bias_ref[0, h], same)
        other = jnp.where(here, chain_bias_ref[1, h], other)
    mask = jnp.zeros(shape, F32)
    for k in range(SUBLANES):
        mask = jnp.where(row == k, mask_ref[0, k].astype(F32), mask)
    bias = bias + jnp.where(key_chain == query_chain, same, other)
    upper = (lane >= cells).astype(jnp.int32)
    tail = jnp.where(upper != far, bias, mask).astype(BF16)
    out_ref[:, block.shape[0] :, :] = jnp.broadcast_to(tail[None], (out_ref.shape[0], *tail.shape))


def block_kernel(
    seq_count, block_ref, row_proj_ref, row_out_far, column_proj_far, column_out_far, expansion_far,
    contraction_far, out_ref, second_ref, one_ref, row_out_ref, column_proj_ref,
    column_out_ref, expansion_ref, contraction_ref, arrived, fence,
):
    far = (row_out_far, column_proj_far, column_out_far, expansion_far, contraction_far)
    near = (row_out_ref, column_proj_ref, column_out_ref, expansion_ref, contraction_ref)
    copies = [
        pltpu.make_async_copy(source, target, arrived.at[k])
        for k, (source, target) in enumerate(zip(far, near))
    ]
    for copy in copies:
        copy.start()
    pl.semaphore_signal(fence, 1)
    pl.semaphore_wait(fence, 1)
    count, rows, _ = block_ref.shape
    far_count, near_count = 2, count // seq_count // 2
    own_rows = SUBLANES
    width = rows * LANES // own_rows - LANES
    parts = width // LANES
    members = far_count * near_count
    residues = seq_count * own_rows
    heads, depth = HEAD_TOTAL, HEAD_DEPTH
    inner = heads * depth
    cells = heads * own_rows
    tokens = members * own_rows
    seq = lax.axis_index("seq")
    me = lax.axis_index("near") * far_count + lax.axis_index("far")
    scaling = depth**-0.5

    def part(ref_index, k):
        return block_ref[ref_index, k * own_rows : (k + 1) * own_rows, :].astype(F32)

    def at(m, s):
        return (m // far_count * seq_count + s) * far_count + m % far_count

    def tail(m, s):
        return block_ref[at(m, s), parts * own_rows :, :].astype(F32)

    def mine(k):
        return jnp.concatenate([part(at(m, seq), k) for m in range(members)], axis=0)

    residual = [mine(k) for k in range(parts)]
    own = jnp.concatenate(normalize(residual, width), axis=1).astype(BF16)
    queries = mm(own, row_proj_ref[:, :inner]).astype(BF16).astype(F32)
    gates = mm(own, row_proj_ref[:, 3 * inner :]).astype(BF16).astype(F32)
    everything = slice(None)
    x = [part(everything, k).reshape(count * own_rows, LANES) for k in range(parts)]
    normed = jnp.concatenate(normalize(x, width), axis=1).astype(BF16)
    all_keys = mm(normed, row_proj_ref[:, inner : 2 * inner]).astype(BF16)
    all_values = mm(normed, row_proj_ref[:, 2 * inner : 3 * inner]).astype(BF16)

    head_of = iota((heads, 1, inner), 2) // depth == iota((heads, 1, inner), 0)
    spread = jnp.where(
        head_of[None], queries.reshape(members, 1, own_rows, inner), 0.0
    ).reshape(members * cells, inner).astype(BF16)

    shape = (own_rows, LANES)
    row, lane = iota(shape, 0), iota(shape, 1)
    lower = lane < cells
    bias = []
    first = row < own_rows // 2
    for m in range(0, members, 2):
        far = m // near_count
        even, odd = (at((n - far * near_count) * far_count + far, seq) for n in (m, m + 1))
        even, odd = (block_ref[n, parts * own_rows :, :].astype(F32) for n in (even, odd))
        both = jnp.where(first, even, odd)
        valid = lower if far else jnp.logical_not(lower)
        bias.append(jnp.where(valid, both, pltpu.roll(both, cells, 1)))
    bias = jnp.concatenate(bias, axis=0)
    wide = iota((residues, LANES), 1) < cells
    keeps = [
        jnp.concatenate(
            [jnp.where(lower, tail(m, s), tail(m + 1, s)) for s in range(seq_count)], axis=0
        ) > 0
        for m in range(0, members, 2)
    ]

    def unmix(two):
        pieces = two.reshape(seq_count, far_count, own_rows, LANES)
        return jnp.where(wide, pieces[:, 0].reshape(wide.shape), pieces[:, 1].reshape(wide.shape))

    def remix(one):
        pieces = [
            half.reshape(seq_count, 1, own_rows, LANES)
            for half in (jnp.where(wide, one, 0.0), jnp.where(wide, 0.0, one))
        ]
        return jnp.concatenate(pieces, axis=1).reshape(2 * residues, LANES)

    scores = [
        lax.dot_general(
            all_keys[m * residues : (m + 2) * residues],
            spread[m * cells : (m + 2) * cells],
            (((1,), (1,)), ((), ())),
            preferred_element_type=F32,
        )
        for m in range(0, members, 2)
    ]
    scores = [unmix(two) * scaling + bias for two in scores]
    scores = [jnp.where(keep, two, -1000000000.0) for two, keep in zip(scores, keeps)]
    scores = [jnp.exp(two - jnp.max(two, axis=0, keepdims=True)) for two in scores]
    weights = [two / jnp.sum(two, axis=0, keepdims=True) for two in scores]
    weights = [remix(two).astype(BF16) for two in weights]
    mixed = [
        lax.dot_general(
            two, all_values[2 * k * residues : 2 * (k + 1) * residues],
            (((0,), (0,)), ((), ())), preferred_element_type=F32,
        )
        for k, two in enumerate(weights)
    ]
    mixed = [
        jnp.sum(jnp.where(head_of[None], two.reshape(2, heads, own_rows, inner), 0.0), axis=1)
        for two in mixed
    ]
    attended = jnp.concatenate(mixed, axis=0).reshape(tokens, inner)
    gated = (jax.nn.sigmoid(gates) * attended).astype(BF16)
    copies[0].wait()
    one = (jnp.concatenate(residual, axis=1) + mm(gated, row_out_ref[...])).astype(BF16).astype(F32)
    one_ref[...] = one.reshape(members, own_rows, width)

    second = normalize_rows(one)
    second_ref[...] = second.reshape(members, own_rows, width)
    copies[1].wait()
    key_values = mm(second, column_proj_ref[:, inner : 3 * inner]).astype(BF16).astype(F32)
    own = second_ref[me]
    queries = mm(own, column_proj_ref[:, :inner]).astype(BF16).astype(F32)
    gates = mm(own, column_proj_ref[:, 3 * inner :]).astype(BF16).astype(F32)
    products = (
        key_values[:, :inner].reshape(members, own_rows, inner) * queries[None]
    ).reshape(tokens, inner)
    high = products.astype(BF16)
    low = (products - high.astype(F32)).astype(BF16)
    same_head = (iota((inner, inner), 0) // depth == iota((inner, inner), 1) // depth).astype(
        F32
    ).astype(BF16)
    scores = (mm(high, same_head) + mm(low, same_head)) * scaling
    scores = scores.reshape(members, own_rows, inner)
    keep = []
    for m in range(members):
        mask = tail(m, seq)
        valid = jnp.logical_not(lower) if m % far_count else lower
        mask = jnp.where(valid, mask, pltpu.roll(mask, cells, 1))
        keep.append(jnp.concatenate([mask] * (inner // LANES), axis=1)[None])
    keep = jnp.concatenate(keep, axis=0)
    scores = jnp.where(keep > 0, scores, -1000000000.0)
    scores = jnp.exp(scores - jnp.max(scores, axis=0, keepdims=True))
    weights = (scores / jnp.sum(scores, axis=0, keepdims=True)).astype(BF16).astype(F32)
    attended = jnp.sum(
        weights * key_values[:, inner:].reshape(members, own_rows, inner), axis=0
    )
    gated = (jax.nn.sigmoid(gates) * attended).astype(BF16)
    copies[2].wait()
    two = one_ref[me] + mm(gated, column_out_ref[...])
    copies[3].wait()
    hidden = jnp.maximum(mm(normalize_rows(two), expansion_ref[...]), 0.0).astype(BF16)
    copies[4].wait()
    out_ref[0] = (two + mm(hidden, contraction_ref[...])).astype(BF16)


def whole_body(
    homolog_tensor,
    pair_features,
    entry_real_mask,
    chain_ids,
    horizontal_matrices,
    horizontal_projector,
    bias_proj,
    chain_bias,
    column_proj,
    vertical_projector,
    expansion_matrix,
    contraction_matrix,
):
    _, own_rows, width = homolog_tensor.shape
    seq_count = lax.axis_size("seq")
    dap_count = lax.axis_size("far") * lax.axis_size("near")
    count = dap_count * seq_count
    rows = own_rows * (width // LANES + 1)
    vmem, hbm = (pl.BlockSpec(memory_space=space) for space in (pltpu.VMEM, pltpu.HBM))
    vectors = [pair_features, bias_proj.T, homolog_tensor]
    scalars = [chain_ids, chain_bias, entry_real_mask]
    packed = pl.pallas_call(
        pack_kernel,
        out_shape=jax.ShapeDtypeStruct((count, rows, LANES), BF16),
        in_specs=[hbm] * len(vectors + scalars),
        out_specs=vmem,
        scratch_shapes=[
            *(pltpu.VMEM(operand.shape, operand.dtype) for operand in vectors),
            *(pltpu.SMEM(operand.shape, operand.dtype) for operand in scalars),
            pltpu.SemaphoreType.DMA((len(vectors + scalars),)),
        ],
        compiler_params=pltpu.CompilerParams(vmem_limit_bytes=8 << 20),
    )(*map(in_hbm, vectors + scalars))
    blocks = lax.all_to_all(packed, ("near", "seq", "far"), split_axis=0, concat_axis=0, tiled=True)
    later = [
        horizontal_projector, column_proj, vertical_projector, expansion_matrix, contraction_matrix
    ]
    return pl.pallas_call(
        lambda *refs: block_kernel(seq_count, *refs),
        out_shape=jax.ShapeDtypeStruct(homolog_tensor.shape, BF16),
        in_specs=[vmem] * 2 + [hbm] * len(later),
        out_specs=vmem,
        scratch_shapes=[
            pltpu.VMEM((dap_count, own_rows, width), BF16),
            pltpu.VMEM((dap_count, own_rows, width), F32),
            *(pltpu.VMEM(weight.shape, weight.dtype) for weight in later),
            pltpu.SemaphoreType.DMA((len(later),)),
            pltpu.SemaphoreType.REGULAR,
        ],
        compiler_params=pltpu.CompilerParams(vmem_limit_bytes=16 << 20),
    )(blocks, horizontal_matrices, *map(in_hbm, later))


def in_hbm(operand):
    return pltpu.with_memory_space_constraint(operand, pltpu.HBM)


def fits_whole(homolog_tensor, pair_features, dap_count, seq_count):
    rows, residues, width = homolog_tensor.shape
    _, _, pair_width = pair_features.shape
    return (
        rows == dap_count
        and residues == seq_count * SUBLANES
        and 2 * residues == dap_count * SUBLANES
        and dap_count % 4 == 0
        and 2 * HEAD_TOTAL * SUBLANES == LANES
        and width % LANES == 0
        and pair_width == LANES
        and HEAD_TOTAL * HEAD_DEPTH % LANES == 0
        and homolog_tensor.size * 2 <= WHOLE_BYTES
    )


def solution(mesh):
    def placed(dap):
        return (P(dap, "seq", None), P("seq", dap, None), P(dap, "seq"), *[P()] * 9)

    def step(*operands):
        dap_count, seq_count = mesh.shape["dap"], mesh.shape["seq"]
        if fits_whole(operands[0], operands[1], dap_count, seq_count):
            devices = mesh.devices.reshape(2, dap_count // 2, seq_count)
            used, chosen, dap = Mesh(devices, ("far", "near", "seq")), whole_body, ("far", "near")
        else:
            used, chosen, dap = mesh, body, "dap"
        return jax.shard_map(
            chosen, mesh=used, in_specs=placed(dap), out_specs=P(dap, "seq", None), check_vma=False
        )(*operands)

    return step
```

```python
import functools

import jax
import jax.numpy as jnp
from jax import lax
from jax.experimental import pallas as pl
from jax.experimental.pallas import tpu as pltpu
from jax.sharding import Mesh, PartitionSpec as P

HEAD_TOTAL = 8
HEAD_DEPTH = 32


epsilon = 1e-05


def layer_norm(inputs):
    center = inputs - jnp.mean(inputs, axis=-1, keepdims=True)
    spread = jnp.mean(center * center, axis=-1, keepdims=True)
    return center * lax.rsqrt(spread + epsilon)


def attend(queries, key_part, value_part, keep_mask, bias_term):
    scores = jnp.einsum(
        "ihd,jhd->hij", queries, key_part, preferred_element_type=jnp.float32
    ) * HEAD_DEPTH ** (-0.5)
    if bias_term is not None:
        scores = scores + bias_term.astype(jnp.float32)
    scores = jnp.where(keep_mask[None, None, :] > 0, scores, -1000000000.0)
    weights = jax.nn.softmax(scores, axis=-1).astype(jnp.bfloat16)
    return jnp.einsum("hij,jhd->ihd", weights, value_part, preferred_element_type=jnp.float32)


def column_update(
    column, keep_column, column_proj, vertical_projector, expansion_matrix, contraction_matrix
):
    expanded_dimension = HEAD_TOTAL * HEAD_DEPTH
    standardized = layer_norm(column.astype(jnp.float32)).astype(jnp.bfloat16)
    projected = jnp.dot(standardized, column_proj, preferred_element_type=jnp.float32).astype(
        jnp.bfloat16
    )
    queries = projected[:, :expanded_dimension].reshape(-1, HEAD_TOTAL, HEAD_DEPTH)
    key_part = projected[:, expanded_dimension : 2 * expanded_dimension].reshape(
        -1, HEAD_TOTAL, HEAD_DEPTH
    )
    value_part = projected[:, 2 * expanded_dimension : 3 * expanded_dimension].reshape(
        -1, HEAD_TOTAL, HEAD_DEPTH
    )
    attended = attend(queries, key_part, value_part, keep_column, None).reshape(
        -1, expanded_dimension
    )
    sigmoid_scaled = (
        jax.nn.sigmoid(projected[:, 3 * expanded_dimension :].astype(jnp.float32)) * attended
    ).astype(jnp.bfloat16)
    mixed = column.astype(jnp.float32) + jnp.dot(
        sigmoid_scaled, vertical_projector, preferred_element_type=jnp.float32
    )
    inner = jnp.maximum(
        jnp.dot(
            layer_norm(mixed).astype(jnp.bfloat16),
            expansion_matrix,
            preferred_element_type=jnp.float32,
        ),
        0.0,
    ).astype(jnp.bfloat16)
    return (mixed + jnp.dot(inner, contraction_matrix, preferred_element_type=jnp.float32)).astype(
        jnp.bfloat16
    )


def body(
    homolog_tensor,
    pair_features,
    entry_real_mask,
    chain_ids,
    horizontal_matrices,
    horizontal_projector,
    bias_proj,
    chain_bias,
    column_proj,
    vertical_projector,
    expansion_matrix,
    contraction_matrix,
):
    row_count, local_residues, channels = homolog_tensor.shape
    expanded_dimension = HEAD_TOTAL * HEAD_DEPTH
    dap_count = lax.axis_size("dap")
    pair_rows, pair_columns, pair_width = pair_features.shape
    normed_pair = layer_norm(pair_features.astype(jnp.float32))
    projected_pair = jnp.einsum(
        "ijc,ch->hij", normed_pair, bias_proj, precision=lax.Precision.HIGHEST
    )
    row_chain = lax.dynamic_slice_in_dim(chain_ids, lax.axis_index("seq") * pair_rows, pair_rows)
    column_chain = lax.dynamic_slice_in_dim(
        chain_ids, lax.axis_index("dap") * pair_columns, pair_columns
    )
    same_chain = (row_chain[:, None] == column_chain[None, :]).astype(jnp.float32)
    chain_term = chain_bias[0][:, None, None] * same_chain + chain_bias[1][:, None, None] * (
        1.0 - same_chain
    )
    local_bias = (projected_pair + chain_term).astype(jnp.bfloat16)
    pair_bias = lax.all_gather(local_bias, "dap", axis=2, tiled=True)
    standardized = layer_norm(homolog_tensor.astype(jnp.float32)).astype(jnp.bfloat16)
    flat = standardized.reshape(-1, channels)
    keep_mask = entry_real_mask.astype(jnp.bfloat16)
    projected = (
        jnp.dot(flat, horizontal_matrices, preferred_element_type=jnp.float32)
        .astype(jnp.bfloat16)
        .reshape(row_count, local_residues, 4 * expanded_dimension)
    )
    queries = projected[..., :expanded_dimension]
    gating = projected[..., 3 * expanded_dimension :]
    key_values, keep_all = (
        lax.all_gather(
            projected[..., expanded_dimension : 3 * expanded_dimension], "seq", axis=1, tiled=True
        ),
        lax.all_gather(keep_mask, "seq", axis=1, tiled=True),
    )

    def one_row(inputs_row):
        row_queries, row_pairs, row_keep = inputs_row
        key_part = row_pairs[:, :expanded_dimension].reshape(-1, HEAD_TOTAL, HEAD_DEPTH)
        value_part = row_pairs[:, expanded_dimension:].reshape(-1, HEAD_TOTAL, HEAD_DEPTH)
        return attend(
            row_queries.reshape(local_residues, HEAD_TOTAL, HEAD_DEPTH),
            key_part,
            value_part,
            row_keep,
            pair_bias,
        ).reshape(local_residues, expanded_dimension)

    attended = lax.map(one_row, (queries, key_values, keep_all))
    sigmoid_scaled = (jax.nn.sigmoid(gating.astype(jnp.float32)) * attended).astype(jnp.bfloat16)
    row_result = jnp.dot(
        sigmoid_scaled.reshape(-1, expanded_dimension),
        horizontal_projector,
        preferred_element_type=jnp.float32,
    ).reshape(row_count, local_residues, channels)
    updated_rows = (homolog_tensor.astype(jnp.float32) + row_result).astype(jnp.bfloat16)
    per_device = local_residues // dap_count
    blocks = updated_rows.reshape(row_count, dap_count, per_device, channels)
    keep_blocks = keep_mask.reshape(row_count, dap_count, per_device)

    def single_column(inputs_col):
        return column_update(
            inputs_col[0],
            inputs_col[1],
            column_proj,
            vertical_projector,
            expansion_matrix,
            contraction_matrix,
        )

    column_block = lax.all_to_all(blocks, "dap", split_axis=1, concat_axis=0, tiled=True)
    column_keep = lax.all_to_all(keep_blocks, "dap", split_axis=1, concat_axis=0, tiled=True)
    inputs_col = (jnp.moveaxis(column_block[:, 0], 1, 0), jnp.moveaxis(column_keep[:, 0], 1, 0))
    output_list = lax.map(single_column, inputs_col)
    mixed = jnp.moveaxis(output_list, 0, 1)[:, None]
    returned = lax.all_to_all(mixed, "dap", split_axis=0, concat_axis=1, tiled=True)
    return returned.reshape(row_count, local_residues, channels)


LANES = 128
SUBLANES = 8
WAIT_FLOPS = 20_000_000_000
WHOLE_BYTES = 1 << 20
F32 = jnp.float32
BF16 = jnp.bfloat16


def mm(a, b):
    return lax.dot_general(a, b, (((1,), (0,)), ((), ())), preferred_element_type=F32)


def iota(shape, axis):
    return lax.broadcasted_iota(jnp.int32, shape, axis)


def normalize(parts, width):
    total = parts[0]
    for part in parts[1:]:
        total = total + part
    mean = jnp.sum(total, axis=-1, keepdims=True) * (1.0 / width)
    center = [part - mean for part in parts]
    total = center[0] * center[0]
    for part in center[1:]:
        total = total + part * part
    scale = lax.rsqrt(jnp.sum(total, axis=-1, keepdims=True) * (1.0 / width) + epsilon)
    return [part * scale for part in center]


def halves(x):
    return [x[:, k : k + LANES] for k in range(0, x.shape[1], LANES)]


def normalize_rows(x):
    return jnp.concatenate(normalize(halves(x), x.shape[1]), axis=1).astype(BF16)


def pack_kernel(*refs):
    count = (len(refs) - 2) // 2
    out_ref, arrived = refs[count], refs[-1]
    near = refs[count + 1 : -1]
    copies = [
        pltpu.make_async_copy(source, target, arrived.at[k])
        for k, (source, target) in enumerate(zip(refs[:count], near))
    ]
    for copy in copies:
        copy.start()
    for copy in copies:
        copy.wait()
    pair_ref, proj_ref, msa_ref, chain_ref, chain_bias_ref, mask_ref = near
    queries, keys, width = pair_ref.shape
    cells = HEAD_TOTAL * queries
    far, seq = lax.axis_index("far"), lax.axis_index("seq")
    dap = far * lax.axis_size("near") + lax.axis_index("near")
    pairs = queries * keys

    block = jnp.concatenate(halves(msa_ref[0].astype(F32)), axis=0).astype(BF16)
    out_ref[:, : block.shape[0], :] = jnp.broadcast_to(block[None], (out_ref.shape[0], *block.shape))

    pair = pair_ref[...].astype(F32).reshape(pairs, width)
    center = pair - jnp.sum(pair, axis=-1, keepdims=True) * (1.0 / width)
    spread = jnp.sum(center * center, axis=-1, keepdims=True) * (1.0 / width)
    shape = (pairs, LANES)
    lane = iota(shape, 1)
    bias = jnp.zeros(shape, F32)
    for h in range(HEAD_TOTAL):
        projected = jnp.sum(center * proj_ref[h : h + 1, :], axis=-1, keepdims=True)
        bias = jnp.where(lane % cells // queries == h, projected, bias)
    bias = bias * lax.rsqrt(spread + epsilon)
    bias = jnp.where(lane % queries == iota(shape, 0) // keys, bias, 0.0)
    bias = jnp.sum(bias.reshape(pairs // SUBLANES, SUBLANES, LANES), axis=0)
    bias = bias + pltpu.roll(bias, keys, 0)

    shape = bias.shape
    row, lane = iota(shape, 0), iota(shape, 1)
    key_chain, query_chain = jnp.zeros(shape, jnp.int32), jnp.zeros(shape, jnp.int32)
    for k in range(keys):
        key_chain = jnp.where(row % keys == k, chain_ref[dap * keys + k], key_chain)
    for k in range(queries):
        query_chain = jnp.where(lane % queries == k, chain_ref[seq * queries + k], query_chain)
    same, other = jnp.zeros(shape, F32), jnp.zeros(shape, F32)
    for h in range(HEAD_TOTAL):
        here = lane % cells // queries == h
        same = jnp.where(here, chain_bias_ref[0, h], same)
        other = jnp.where(here, chain_bias_ref[1, h], other)
    mask = jnp.zeros(shape, F32)
    for k in range(SUBLANES):
        mask = jnp.where(row == k, mask_ref[0, k].astype(F32), mask)
    bias = bias + jnp.where(key_chain == query_chain, same, other)
    upper = (lane >= cells).astype(jnp.int32)
    tail = jnp.where(upper != far, bias, mask).astype(BF16)
    out_ref[:, block.shape[0] :, :] = jnp.broadcast_to(tail[None], (out_ref.shape[0], *tail.shape))


def block_kernel(
    seq_count, block_ref, row_proj_ref, row_out_ref, column_proj_ref, column_out_ref, expansion_ref,
    contraction_ref, out_ref, normed_ref, second_ref, one_ref,
):
    count, rows, _ = block_ref.shape
    far_count, near_count = 2, count // seq_count // 2
    own_rows = SUBLANES
    width = rows * LANES // own_rows - LANES
    parts = width // LANES
    members = far_count * near_count
    residues = seq_count * own_rows
    heads, depth = HEAD_TOTAL, HEAD_DEPTH
    inner = heads * depth
    cells = heads * own_rows
    tokens = members * own_rows
    seq = lax.axis_index("seq")
    me = lax.axis_index("near") * far_count + lax.axis_index("far")
    scaling = depth**-0.5

    def part(ref_index, k):
        return block_ref[ref_index, k * own_rows : (k + 1) * own_rows, :].astype(F32)

    def at(m, s):
        return (m // far_count * seq_count + s) * far_count + m % far_count

    def tail(m, s):
        return block_ref[at(m, s), parts * own_rows :, :].astype(F32)

    def mine(k):
        return jnp.concatenate([part(at(m, seq), k) for m in range(members)], axis=0)

    residual = [mine(k) for k in range(parts)]
    everything = slice(None)
    x = [part(everything, k).reshape(count * own_rows, LANES) for k in range(parts)]
    normed = jnp.concatenate(normalize(x, width), axis=1).astype(BF16)
    normed_ref[...] = normed.reshape(near_count, seq_count, far_count * own_rows, width)
    own = normed_ref[:, seq].reshape(tokens, width)
    queries = mm(own, row_proj_ref[:, :inner]).astype(BF16).astype(F32)
    gates = mm(own, row_proj_ref[:, 3 * inner :]).astype(BF16).astype(F32)
    all_keys = mm(normed, row_proj_ref[:, inner : 2 * inner]).astype(BF16)
    all_values = mm(normed, row_proj_ref[:, 2 * inner : 3 * inner]).astype(BF16)

    head_of = iota((heads, 1, inner), 2) // depth == iota((heads, 1, inner), 0)
    spread = jnp.where(
        head_of[None], queries.reshape(members, 1, own_rows, inner), 0.0
    ).reshape(members * cells, inner).astype(BF16)

    shape = (own_rows, LANES)
    row, lane = iota(shape, 0), iota(shape, 1)
    lower = lane < cells
    bias = []
    first = row < own_rows // 2
    for m in range(0, members, 2):
        far = m // near_count
        even, odd = (at((n - far * near_count) * far_count + far, seq) for n in (m, m + 1))
        even, odd = (block_ref[n, parts * own_rows :, :].astype(F32) for n in (even, odd))
        both = jnp.where(first, even, odd)
        valid = lower if far else jnp.logical_not(lower)
        bias.append(jnp.where(valid, both, pltpu.roll(both, cells, 1)))
    bias = jnp.concatenate(bias, axis=0)
    wide = iota((residues, LANES), 1) < cells
    keeps = [
        jnp.concatenate(
            [jnp.where(lower, tail(m, s), tail(m + 1, s)) for s in range(seq_count)], axis=0
        ) > 0
        for m in range(0, members, 2)
    ]

    def unmix(two):
        pieces = two.reshape(seq_count, far_count, own_rows, LANES)
        return jnp.where(wide, pieces[:, 0].reshape(wide.shape), pieces[:, 1].reshape(wide.shape))

    def remix(one):
        pieces = [
            half.reshape(seq_count, 1, own_rows, LANES)
            for half in (jnp.where(wide, one, 0.0), jnp.where(wide, 0.0, one))
        ]
        return jnp.concatenate(pieces, axis=1).reshape(2 * residues, LANES)

    scores = [
        lax.dot_general(
            all_keys[m * residues : (m + 2) * residues],
            spread[m * cells : (m + 2) * cells],
            (((1,), (1,)), ((), ())),
            preferred_element_type=F32,
        )
        for m in range(0, members, 2)
    ]
    scores = [unmix(two) * scaling + bias for two in scores]
    scores = [jnp.where(keep, two, -1000000000.0) for two, keep in zip(scores, keeps)]
    scores = [jnp.exp(two - jnp.max(two, axis=0, keepdims=True)) for two in scores]
    weights = [two * (1.0 / jnp.sum(two, axis=0, keepdims=True)) for two in scores]
    weights = [remix(two).astype(BF16) for two in weights]
    mixed = [
        lax.dot_general(
            two, all_values[2 * k * residues : 2 * (k + 1) * residues],
            (((0,), (0,)), ((), ())), preferred_element_type=F32,
        )
        for k, two in enumerate(weights)
    ]
    mixed = [
        jnp.sum(jnp.where(head_of[None], two.reshape(2, heads, own_rows, inner), 0.0), axis=1)
        for two in mixed
    ]
    attended = jnp.concatenate(mixed, axis=0).reshape(tokens, inner)
    gated = (jax.nn.sigmoid(gates) * attended).astype(BF16)
    one = (jnp.concatenate(residual, axis=1) + mm(gated, row_out_ref[...])).astype(BF16).astype(F32)
    one_ref[...] = one.reshape(members, own_rows, width)

    second = normalize_rows(one)
    second_ref[...] = second.reshape(members, own_rows, width)
    key_values = mm(second, column_proj_ref[:, inner : 3 * inner]).astype(BF16).astype(F32)
    own = second_ref[me]
    queries = mm(own, column_proj_ref[:, :inner]).astype(BF16).astype(F32)
    gates = mm(own, column_proj_ref[:, 3 * inner :]).astype(BF16).astype(F32)
    products = (
        key_values[:, :inner].reshape(members, own_rows, inner) * queries[None]
    ).reshape(tokens, inner)
    high = products.astype(BF16)
    low = (products - high.astype(F32)).astype(BF16)
    same_head = (iota((inner, inner), 0) // depth == iota((inner, inner), 1) // depth).astype(
        F32
    ).astype(BF16)
    scores = (mm(high, same_head) + mm(low, same_head)) * scaling
    scores = scores.reshape(members, own_rows, inner)
    keep = []
    for m in range(members):
        mask = tail(m, seq)
        valid = jnp.logical_not(lower) if m % far_count else lower
        mask = jnp.where(valid, mask, pltpu.roll(mask, cells, 1))
        keep.append(jnp.concatenate([mask] * (inner // LANES), axis=1)[None])
    keep = jnp.concatenate(keep, axis=0)
    scores = jnp.where(keep > 0, scores, -1000000000.0)
    scores = jnp.exp(scores - jnp.max(scores, axis=0, keepdims=True))
    weights = (scores * (1.0 / jnp.sum(scores, axis=0, keepdims=True))).astype(BF16).astype(F32)
    attended = jnp.sum(
        weights * key_values[:, inner:].reshape(members, own_rows, inner), axis=0
    )
    gated = (jax.nn.sigmoid(gates) * attended).astype(BF16)
    two = one_ref[me] + mm(gated, column_out_ref[...])
    hidden = jnp.maximum(mm(normalize_rows(two), expansion_ref[...]), 0.0).astype(BF16)
    out_ref[0] = (two + mm(hidden, contraction_ref[...])).astype(BF16)


def whole_body(
    homolog_tensor,
    pair_features,
    entry_real_mask,
    chain_ids,
    horizontal_matrices,
    horizontal_projector,
    bias_proj,
    chain_bias,
    column_proj,
    vertical_projector,
    expansion_matrix,
    contraction_matrix,
):
    _, own_rows, width = homolog_tensor.shape
    seq_count = lax.axis_size("seq")
    dap_count = lax.axis_size("far") * lax.axis_size("near")
    count = dap_count * seq_count
    rows = own_rows * (width // LANES + 1)
    vmem, hbm = (pl.BlockSpec(memory_space=space) for space in (pltpu.VMEM, pltpu.HBM))
    vectors = [pair_features, bias_proj.T, homolog_tensor]
    scalars = [chain_ids, chain_bias, entry_real_mask]
    packed = pl.pallas_call(
        pack_kernel,
        out_shape=jax.ShapeDtypeStruct((count, rows, LANES), BF16),
        in_specs=[hbm] * len(vectors + scalars),
        out_specs=vmem,
        scratch_shapes=[
            *(pltpu.VMEM(operand.shape, operand.dtype) for operand in vectors),
            *(pltpu.SMEM(operand.shape, operand.dtype) for operand in scalars),
            pltpu.SemaphoreType.DMA((len(vectors + scalars),)),
        ],
        compiler_params=pltpu.CompilerParams(vmem_limit_bytes=8 << 20),
        cost_estimate=pl.CostEstimate(flops=WAIT_FLOPS, bytes_accessed=count * rows * LANES * 2, transcendentals=0),
    )(*map(in_hbm, vectors + scalars))
    blocks = lax.all_to_all(packed, ("near", "seq", "far"), split_axis=0, concat_axis=0, tiled=True)
    return pl.pallas_call(
        functools.partial(block_kernel, seq_count),
        out_shape=jax.ShapeDtypeStruct(homolog_tensor.shape, BF16),
        in_specs=[vmem] * 7,
        out_specs=vmem,
        scratch_shapes=[
            pltpu.VMEM((dap_count // 2, seq_count, 2 * own_rows, width), BF16),
            pltpu.VMEM((dap_count, own_rows, width), BF16),
            pltpu.VMEM((dap_count, own_rows, width), F32),
        ],
        compiler_params=pltpu.CompilerParams(vmem_limit_bytes=16 << 20),
    )(
        blocks,
        horizontal_matrices,
        horizontal_projector,
        column_proj,
        vertical_projector,
        expansion_matrix,
        contraction_matrix,
    )


def in_hbm(operand):
    return pltpu.with_memory_space_constraint(operand, pltpu.HBM)


def fits_whole(homolog_tensor, pair_features, dap_count, seq_count):
    rows, residues, width = homolog_tensor.shape
    _, _, pair_width = pair_features.shape
    return (
        rows == dap_count
        and residues == seq_count * SUBLANES
        and 2 * residues == dap_count * SUBLANES
        and dap_count % 4 == 0
        and 2 * HEAD_TOTAL * SUBLANES == LANES
        and width % LANES == 0
        and pair_width == LANES
        and HEAD_TOTAL * HEAD_DEPTH % LANES == 0
        and homolog_tensor.size * 2 <= WHOLE_BYTES
    )


def solution(mesh):
    def placed(dap):
        return (P(dap, "seq", None), P("seq", dap, None), P(dap, "seq"), *[P()] * 9)

    def step(*operands):
        dap_count, seq_count = mesh.shape["dap"], mesh.shape["seq"]
        if fits_whole(operands[0], operands[1], dap_count, seq_count):
            devices = mesh.devices.reshape(2, dap_count // 2, seq_count)
            used, chosen, dap = Mesh(devices, ("far", "near", "seq")), whole_body, ("far", "near")
        else:
            used, chosen, dap = mesh, body, "dap"
        return jax.shard_map(
            chosen, mesh=used, in_specs=placed(dap), out_specs=P(dap, "seq", None), check_vma=False
        )(*operands)

    return step
```

```python
import functools

import jax
import jax.numpy as jnp
from jax import lax
from jax.experimental import pallas as pl
from jax.experimental.pallas import tpu as pltpu
from jax.sharding import Mesh, PartitionSpec as P

HEAD_TOTAL = 8
HEAD_DEPTH = 32


epsilon = 1e-05


def layer_norm(inputs):
    center = inputs - jnp.mean(inputs, axis=-1, keepdims=True)
    spread = jnp.mean(center * center, axis=-1, keepdims=True)
    return center * lax.rsqrt(spread + epsilon)


def attend(queries, key_part, value_part, keep_mask, bias_term):
    scores = jnp.einsum(
        "ihd,jhd->hij", queries, key_part, preferred_element_type=jnp.float32
    ) * HEAD_DEPTH ** (-0.5)
    if bias_term is not None:
        scores = scores + bias_term.astype(jnp.float32)
    scores = jnp.where(keep_mask[None, None, :] > 0, scores, -1000000000.0)
    weights = jax.nn.softmax(scores, axis=-1).astype(jnp.bfloat16)
    return jnp.einsum("hij,jhd->ihd", weights, value_part, preferred_element_type=jnp.float32)


def column_update(
    column, keep_column, column_proj, vertical_projector, expansion_matrix, contraction_matrix
):
    expanded_dimension = HEAD_TOTAL * HEAD_DEPTH
    standardized = layer_norm(column.astype(jnp.float32)).astype(jnp.bfloat16)
    projected = jnp.dot(standardized, column_proj, preferred_element_type=jnp.float32).astype(
        jnp.bfloat16
    )
    queries = projected[:, :expanded_dimension].reshape(-1, HEAD_TOTAL, HEAD_DEPTH)
    key_part = projected[:, expanded_dimension : 2 * expanded_dimension].reshape(
        -1, HEAD_TOTAL, HEAD_DEPTH
    )
    value_part = projected[:, 2 * expanded_dimension : 3 * expanded_dimension].reshape(
        -1, HEAD_TOTAL, HEAD_DEPTH
    )
    attended = attend(queries, key_part, value_part, keep_column, None).reshape(
        -1, expanded_dimension
    )
    sigmoid_scaled = (
        jax.nn.sigmoid(projected[:, 3 * expanded_dimension :].astype(jnp.float32)) * attended
    ).astype(jnp.bfloat16)
    mixed = column.astype(jnp.float32) + jnp.dot(
        sigmoid_scaled, vertical_projector, preferred_element_type=jnp.float32
    )
    inner = jnp.maximum(
        jnp.dot(
            layer_norm(mixed).astype(jnp.bfloat16),
            expansion_matrix,
            preferred_element_type=jnp.float32,
        ),
        0.0,
    ).astype(jnp.bfloat16)
    return (mixed + jnp.dot(inner, contraction_matrix, preferred_element_type=jnp.float32)).astype(
        jnp.bfloat16
    )


def body(
    homolog_tensor,
    pair_features,
    entry_real_mask,
    chain_ids,
    horizontal_matrices,
    horizontal_projector,
    bias_proj,
    chain_bias,
    column_proj,
    vertical_projector,
    expansion_matrix,
    contraction_matrix,
):
    row_count, local_residues, channels = homolog_tensor.shape
    expanded_dimension = HEAD_TOTAL * HEAD_DEPTH
    dap_count = lax.axis_size("dap")
    pair_rows, pair_columns, pair_width = pair_features.shape
    normed_pair = layer_norm(pair_features.astype(jnp.float32))
    projected_pair = jnp.einsum(
        "ijc,ch->hij", normed_pair, bias_proj, precision=lax.Precision.HIGHEST
    )
    row_chain = lax.dynamic_slice_in_dim(chain_ids, lax.axis_index("seq") * pair_rows, pair_rows)
    column_chain = lax.dynamic_slice_in_dim(
        chain_ids, lax.axis_index("dap") * pair_columns, pair_columns
    )
    same_chain = (row_chain[:, None] == column_chain[None, :]).astype(jnp.float32)
    chain_term = chain_bias[0][:, None, None] * same_chain + chain_bias[1][:, None, None] * (
        1.0 - same_chain
    )
    local_bias = (projected_pair + chain_term).astype(jnp.bfloat16)
    pair_bias = lax.all_gather(local_bias, "dap", axis=2, tiled=True)
    standardized = layer_norm(homolog_tensor.astype(jnp.float32)).astype(jnp.bfloat16)
    flat = standardized.reshape(-1, channels)
    keep_mask = entry_real_mask.astype(jnp.bfloat16)
    projected = (
        jnp.dot(flat, horizontal_matrices, preferred_element_type=jnp.float32)
        .astype(jnp.bfloat16)
        .reshape(row_count, local_residues, 4 * expanded_dimension)
    )
    queries = projected[..., :expanded_dimension]
    gating = projected[..., 3 * expanded_dimension :]
    key_values, keep_all = (
        lax.all_gather(
            projected[..., expanded_dimension : 3 * expanded_dimension], "seq", axis=1, tiled=True
        ),
        lax.all_gather(keep_mask, "seq", axis=1, tiled=True),
    )

    def one_row(inputs_row):
        row_queries, row_pairs, row_keep = inputs_row
        key_part = row_pairs[:, :expanded_dimension].reshape(-1, HEAD_TOTAL, HEAD_DEPTH)
        value_part = row_pairs[:, expanded_dimension:].reshape(-1, HEAD_TOTAL, HEAD_DEPTH)
        return attend(
            row_queries.reshape(local_residues, HEAD_TOTAL, HEAD_DEPTH),
            key_part,
            value_part,
            row_keep,
            pair_bias,
        ).reshape(local_residues, expanded_dimension)

    attended = lax.map(one_row, (queries, key_values, keep_all))
    sigmoid_scaled = (jax.nn.sigmoid(gating.astype(jnp.float32)) * attended).astype(jnp.bfloat16)
    row_result = jnp.dot(
        sigmoid_scaled.reshape(-1, expanded_dimension),
        horizontal_projector,
        preferred_element_type=jnp.float32,
    ).reshape(row_count, local_residues, channels)
    updated_rows = (homolog_tensor.astype(jnp.float32) + row_result).astype(jnp.bfloat16)
    per_device = local_residues // dap_count
    blocks = updated_rows.reshape(row_count, dap_count, per_device, channels)
    keep_blocks = keep_mask.reshape(row_count, dap_count, per_device)

    def single_column(inputs_col):
        return column_update(
            inputs_col[0],
            inputs_col[1],
            column_proj,
            vertical_projector,
            expansion_matrix,
            contraction_matrix,
        )

    column_block = lax.all_to_all(blocks, "dap", split_axis=1, concat_axis=0, tiled=True)
    column_keep = lax.all_to_all(keep_blocks, "dap", split_axis=1, concat_axis=0, tiled=True)
    inputs_col = (jnp.moveaxis(column_block[:, 0], 1, 0), jnp.moveaxis(column_keep[:, 0], 1, 0))
    output_list = lax.map(single_column, inputs_col)
    mixed = jnp.moveaxis(output_list, 0, 1)[:, None]
    returned = lax.all_to_all(mixed, "dap", split_axis=0, concat_axis=1, tiled=True)
    return returned.reshape(row_count, local_residues, channels)


LANES = 128
SUBLANES = 8
WAIT_FLOPS = 20_000_000_000
WHOLE_BYTES = 1 << 20
F32 = jnp.float32
BF16 = jnp.bfloat16


def mm(a, b):
    return lax.dot_general(a, b, (((1,), (0,)), ((), ())), preferred_element_type=F32)


def iota(shape, axis):
    return lax.broadcasted_iota(jnp.int32, shape, axis)


def normalize(parts, width):
    total = parts[0]
    for part in parts[1:]:
        total = total + part
    mean = jnp.sum(total, axis=-1, keepdims=True) * (1.0 / width)
    center = [part - mean for part in parts]
    total = center[0] * center[0]
    for part in center[1:]:
        total = total + part * part
    scale = lax.rsqrt(jnp.sum(total, axis=-1, keepdims=True) * (1.0 / width) + epsilon)
    return [part * scale for part in center]


def halves(x):
    return [x[:, k : k + LANES] for k in range(0, x.shape[1], LANES)]


def normalize_rows(x):
    return jnp.concatenate(normalize(halves(x), x.shape[1]), axis=1).astype(BF16)


def pack_kernel(*refs):
    count = (len(refs) - 2) // 2
    out_ref, arrived = refs[count], refs[-1]
    near = refs[count + 1 : -1]
    copies = [
        pltpu.make_async_copy(source, target, arrived.at[k])
        for k, (source, target) in enumerate(zip(refs[:count], near))
    ]
    for copy in copies:
        copy.start()
    for copy in copies:
        copy.wait()
    pair_ref, proj_ref, msa_ref, chain_ref, chain_bias_ref, mask_ref = near
    queries, keys, width = pair_ref.shape
    cells = HEAD_TOTAL * queries
    far, seq = lax.axis_index("far"), lax.axis_index("seq")
    dap = far * lax.axis_size("near") + lax.axis_index("near")
    pairs = queries * keys

    def spread_out(k, piece):
        out_ref[:, k] = jnp.broadcast_to(piece.astype(BF16)[None], (out_ref.shape[0], *piece.shape))

    block = jnp.concatenate(halves(msa_ref[0].astype(F32)), axis=0)
    for k in range(block.shape[0] // keys):
        spread_out(k, block[k * keys : (k + 1) * keys])

    pair = pair_ref[...].astype(F32).reshape(pairs, width)
    center = pair - jnp.sum(pair, axis=-1, keepdims=True) * (1.0 / width)
    spread = jnp.sum(center * center, axis=-1, keepdims=True) * (1.0 / width)
    shape = (pairs, LANES)
    lane = iota(shape, 1)
    bias = jnp.zeros(shape, F32)
    for h in range(HEAD_TOTAL):
        projected = jnp.sum(center * proj_ref[h : h + 1, :], axis=-1, keepdims=True)
        bias = jnp.where(lane % cells // queries == h, projected, bias)
    bias = bias * lax.rsqrt(spread + epsilon)
    bias = jnp.where(lane % queries == iota(shape, 0) // keys, bias, 0.0)
    bias = jnp.sum(bias.reshape(pairs // SUBLANES, SUBLANES, LANES), axis=0)
    bias = bias + pltpu.roll(bias, keys, 0)

    shape = bias.shape
    row, lane = iota(shape, 0), iota(shape, 1)
    key_chain, query_chain = jnp.zeros(shape, jnp.int32), jnp.zeros(shape, jnp.int32)
    for k in range(keys):
        key_chain = jnp.where(row % keys == k, chain_ref[dap * keys + k], key_chain)
    for k in range(queries):
        query_chain = jnp.where(lane % queries == k, chain_ref[seq * queries + k], query_chain)
    same, other = jnp.zeros(shape, F32), jnp.zeros(shape, F32)
    for h in range(HEAD_TOTAL):
        here = lane % cells // queries == h
        same = jnp.where(here, chain_bias_ref[0, h], same)
        other = jnp.where(here, chain_bias_ref[1, h], other)
    mask = jnp.zeros(shape, F32)
    for k in range(SUBLANES):
        mask = jnp.where(row == k, mask_ref[0, k].astype(F32), mask)
    bias = bias + jnp.where(key_chain == query_chain, same, other)
    mask = jnp.where(lane == 0, mask, jnp.where(lane == 1, pltpu.roll(mask, keys, 0), 0.0))
    spread_out(block.shape[0] // keys, jnp.where(lane >= cells, bias, mask)[:keys])


def block_kernel(
    seq_count, block_ref, row_proj_ref, row_out_ref, column_proj_ref, column_out_ref, expansion_ref,
    contraction_ref, out_ref, normed_ref, second_ref, one_ref,
):
    count, pieces, rows, _ = block_ref.shape
    far_count, near_count = 2, count // seq_count // 2
    own_rows = SUBLANES
    width = (pieces - 1) * rows * LANES // own_rows
    parts = width // LANES
    members = far_count * near_count
    residues = seq_count * own_rows
    heads, depth = HEAD_TOTAL, HEAD_DEPTH
    inner = heads * depth
    cells = heads * own_rows
    tokens = members * own_rows
    seq = lax.axis_index("seq")
    me = lax.axis_index("near") * far_count + lax.axis_index("far")
    scaling = depth**-0.5

    def part(ref_index, k):
        halves_of = [block_ref[ref_index, 2 * k + n].astype(F32) for n in range(2)]
        return jnp.concatenate(halves_of, axis=-2)

    def at(m, s):
        return (m // far_count * seq_count + s) * far_count + m % far_count

    def mine(k):
        return jnp.concatenate([part(at(m, seq), k) for m in range(members)], axis=0)

    residual = [mine(k) for k in range(parts)]
    everything = slice(None)
    x = [part(everything, k).reshape(count * own_rows, LANES) for k in range(parts)]
    normed = jnp.concatenate(normalize(x, width), axis=1).astype(BF16)
    normed_ref[...] = normed.reshape(near_count, seq_count, far_count * own_rows, width)
    own = normed_ref[:, seq].reshape(tokens, width)
    queries = mm(own, row_proj_ref[:, :inner]).astype(BF16).astype(F32)
    gates = mm(own, row_proj_ref[:, 3 * inner :]).astype(BF16).astype(F32)
    all_keys = mm(normed, row_proj_ref[:, inner : 2 * inner]).astype(BF16)
    all_values = mm(normed, row_proj_ref[:, 2 * inner : 3 * inner]).astype(BF16)

    head_of = iota((heads, 1, inner), 2) // depth == iota((heads, 1, inner), 0)
    spread = jnp.where(
        head_of[None], queries.reshape(members, 1, own_rows, inner), 0.0
    ).reshape(members * cells, inner).astype(BF16)

    shape = (own_rows, LANES)
    row, lane = iota(shape, 0), iota(shape, 1)
    lower = lane < cells
    bias = []
    tails = block_ref[:, pieces - 1].astype(F32).reshape(count * rows, LANES).astype(BF16)
    taken = iota((LANES, 2 * LANES), 0) == iota((LANES, 2 * LANES), 1) // LANES
    masks = mm(tails, taken.astype(F32).astype(BF16))
    masks = [half.reshape(count, rows, LANES) for half in halves(masks)]
    masks = jnp.concatenate(masks, axis=1)
    for m in range(0, members, 2):
        far = m // near_count
        even, odd = (at((n - far * near_count) * far_count + far, seq) for n in (m, m + 1))
        both = [block_ref[n, pieces - 1].astype(F32) for n in (even, odd)]
        both = jnp.concatenate(both, axis=0)
        bias.append(jnp.where(lower, pltpu.roll(both, cells, 1), both))
    bias = jnp.concatenate(bias, axis=0)
    wide = iota((residues, LANES), 1) < cells
    keeps = [
        jnp.concatenate(
            [jnp.where(lower, masks[at(m, s)], masks[at(m + 1, s)]) for s in range(seq_count)],
            axis=0,
        ) > 0
        for m in range(0, members, 2)
    ]

    def unmix(two):
        pieces = two.reshape(seq_count, far_count, own_rows, LANES)
        return jnp.where(wide, pieces[:, 0].reshape(wide.shape), pieces[:, 1].reshape(wide.shape))

    def remix(one):
        pieces = [
            half.reshape(seq_count, 1, own_rows, LANES)
            for half in (jnp.where(wide, one, 0.0), jnp.where(wide, 0.0, one))
        ]
        return jnp.concatenate(pieces, axis=1).reshape(2 * residues, LANES)

    scores = [
        lax.dot_general(
            all_keys[m * residues : (m + 2) * residues],
            spread[m * cells : (m + 2) * cells],
            (((1,), (1,)), ((), ())),
            preferred_element_type=F32,
        )
        for m in range(0, members, 2)
    ]
    scores = [unmix(two) * scaling + bias for two in scores]
    scores = [jnp.where(keep, two, -1000000000.0) for two, keep in zip(scores, keeps)]
    scores = [jnp.exp(two - jnp.max(two, axis=0, keepdims=True)) for two in scores]
    weights = [two * (1.0 / jnp.sum(two, axis=0, keepdims=True)) for two in scores]
    weights = [remix(two).astype(BF16) for two in weights]
    mixed = [
        lax.dot_general(
            two, all_values[2 * k * residues : 2 * (k + 1) * residues],
            (((0,), (0,)), ((), ())), preferred_element_type=F32,
        )
        for k, two in enumerate(weights)
    ]
    mixed = [
        jnp.sum(jnp.where(head_of[None], two.reshape(2, heads, own_rows, inner), 0.0), axis=1)
        for two in mixed
    ]
    attended = jnp.concatenate(mixed, axis=0).reshape(tokens, inner)
    gated = (jax.nn.sigmoid(gates) * attended).astype(BF16)
    one = (jnp.concatenate(residual, axis=1) + mm(gated, row_out_ref[...])).astype(BF16).astype(F32)
    one_ref[...] = one.reshape(members, own_rows, width)

    second = normalize_rows(one)
    second_ref[...] = second.reshape(members, own_rows, width)
    key_values = mm(second, column_proj_ref[:, inner : 3 * inner]).astype(BF16).astype(F32)
    own = second_ref[me]
    queries = mm(own, column_proj_ref[:, :inner]).astype(BF16).astype(F32)
    gates = mm(own, column_proj_ref[:, 3 * inner :]).astype(BF16).astype(F32)
    products = (
        key_values[:, :inner].reshape(members, own_rows, inner) * queries[None]
    ).reshape(tokens, inner)
    high = products.astype(BF16)
    low = (products - high.astype(F32)).astype(BF16)
    same_head = (iota((inner, inner), 0) // depth == iota((inner, inner), 1) // depth).astype(
        F32
    ).astype(BF16)
    scores = (mm(high, same_head) + mm(low, same_head)) * scaling
    scores = scores.reshape(members, own_rows, inner)
    keep = []
    for m in range(members):
        mask = masks[at(m, 0)]
        for s in range(1, seq_count):
            mask = jnp.where(seq == s, masks[at(m, s)], mask)
        keep.append(jnp.concatenate([mask] * (inner // LANES), axis=1)[None])
    keep = jnp.concatenate(keep, axis=0)
    scores = jnp.where(keep > 0, scores, -1000000000.0)
    scores = jnp.exp(scores - jnp.max(scores, axis=0, keepdims=True))
    weights = (scores * (1.0 / jnp.sum(scores, axis=0, keepdims=True))).astype(BF16).astype(F32)
    attended = jnp.sum(
        weights * key_values[:, inner:].reshape(members, own_rows, inner), axis=0
    )
    gated = (jax.nn.sigmoid(gates) * attended).astype(BF16)
    two = one_ref[me] + mm(gated, column_out_ref[...])
    hidden = jnp.maximum(mm(normalize_rows(two), expansion_ref[...]), 0.0).astype(BF16)
    out_ref[0] = (two + mm(hidden, contraction_ref[...])).astype(BF16)


def whole_body(
    homolog_tensor,
    pair_features,
    entry_real_mask,
    chain_ids,
    horizontal_matrices,
    horizontal_projector,
    bias_proj,
    chain_bias,
    column_proj,
    vertical_projector,
    expansion_matrix,
    contraction_matrix,
):
    _, own_rows, width = homolog_tensor.shape
    seq_count = lax.axis_size("seq")
    dap_count = lax.axis_size("far") * lax.axis_size("near")
    count = dap_count * seq_count
    rows = own_rows // 2
    pieces = 2 * width // LANES + 1
    vmem, hbm = (pl.BlockSpec(memory_space=space) for space in (pltpu.VMEM, pltpu.HBM))
    vectors = [pair_features, bias_proj.T, homolog_tensor]
    scalars = [chain_ids, chain_bias, entry_real_mask]
    packed = pl.pallas_call(
        pack_kernel,
        out_shape=jax.ShapeDtypeStruct((count, pieces, rows, LANES), BF16),
        in_specs=[hbm] * len(vectors + scalars),
        out_specs=vmem,
        scratch_shapes=[
            *(pltpu.VMEM(operand.shape, operand.dtype) for operand in vectors),
            *(pltpu.SMEM(operand.shape, operand.dtype) for operand in scalars),
            pltpu.SemaphoreType.DMA((len(vectors + scalars),)),
        ],
        compiler_params=pltpu.CompilerParams(vmem_limit_bytes=8 << 20),
        cost_estimate=pl.CostEstimate(flops=WAIT_FLOPS, bytes_accessed=count * pieces * rows * LANES * 2, transcendentals=0),
    )(*map(in_hbm, vectors + scalars))
    blocks = lax.all_to_all(packed, ("near", "seq", "far"), split_axis=0, concat_axis=0, tiled=True)
    return pl.pallas_call(
        functools.partial(block_kernel, seq_count),
        out_shape=jax.ShapeDtypeStruct(homolog_tensor.shape, BF16),
        in_specs=[vmem] * 7,
        out_specs=vmem,
        scratch_shapes=[
            pltpu.VMEM((dap_count // 2, seq_count, 2 * own_rows, width), BF16),
            pltpu.VMEM((dap_count, own_rows, width), BF16),
            pltpu.VMEM((dap_count, own_rows, width), F32),
        ],
        compiler_params=pltpu.CompilerParams(vmem_limit_bytes=16 << 20),
    )(
        blocks,
        horizontal_matrices,
        horizontal_projector,
        column_proj,
        vertical_projector,
        expansion_matrix,
        contraction_matrix,
    )


def in_hbm(operand):
    return pltpu.with_memory_space_constraint(operand, pltpu.HBM)


def fits_whole(homolog_tensor, pair_features, dap_count, seq_count):
    rows, residues, width = homolog_tensor.shape
    _, _, pair_width = pair_features.shape
    return (
        rows == dap_count
        and residues == seq_count * SUBLANES
        and 2 * residues == dap_count * SUBLANES
        and dap_count % 4 == 0
        and 2 * HEAD_TOTAL * SUBLANES == LANES
        and width % LANES == 0
        and pair_width == LANES
        and HEAD_TOTAL * HEAD_DEPTH % LANES == 0
        and homolog_tensor.size * 2 <= WHOLE_BYTES
    )


def solution(mesh):
    def placed(dap):
        return (P(dap, "seq", None), P("seq", dap, None), P(dap, "seq"), *[P()] * 9)

    def step(*operands):
        dap_count, seq_count = mesh.shape["dap"], mesh.shape["seq"]
        if fits_whole(operands[0], operands[1], dap_count, seq_count):
            devices = mesh.devices.reshape(2, dap_count // 2, seq_count)
            used, chosen, dap = Mesh(devices, ("far", "near", "seq")), whole_body, ("far", "near")
        else:
            used, chosen, dap = mesh, body, "dap"
        return jax.shard_map(
            chosen, mesh=used, in_specs=placed(dap), out_specs=P(dap, "seq", None), check_vma=False
        )(*operands)

    return step
```

```python
import functools

import jax
import jax.numpy as jnp
from jax import lax
from jax.experimental import pallas as pl
from jax.experimental.pallas import tpu as pltpu
from jax.sharding import Mesh, PartitionSpec as P

HEAD_TOTAL = 8
HEAD_DEPTH = 32


epsilon = 1e-05


def layer_norm(inputs):
    center = inputs - jnp.mean(inputs, axis=-1, keepdims=True)
    spread = jnp.mean(center * center, axis=-1, keepdims=True)
    return center * lax.rsqrt(spread + epsilon)


def attend(queries, key_part, value_part, keep_mask, bias_term):
    scores = jnp.einsum(
        "ihd,jhd->hij", queries, key_part, preferred_element_type=jnp.float32
    ) * HEAD_DEPTH ** (-0.5)
    if bias_term is not None:
        scores = scores + bias_term.astype(jnp.float32)
    scores = jnp.where(keep_mask[None, None, :] > 0, scores, -1000000000.0)
    weights = jax.nn.softmax(scores, axis=-1).astype(jnp.bfloat16)
    return jnp.einsum("hij,jhd->ihd", weights, value_part, preferred_element_type=jnp.float32)


def column_update(
    column, keep_column, column_proj, vertical_projector, expansion_matrix, contraction_matrix
):
    expanded_dimension = HEAD_TOTAL * HEAD_DEPTH
    standardized = layer_norm(column.astype(jnp.float32)).astype(jnp.bfloat16)
    projected = jnp.dot(standardized, column_proj, preferred_element_type=jnp.float32).astype(
        jnp.bfloat16
    )
    queries = projected[:, :expanded_dimension].reshape(-1, HEAD_TOTAL, HEAD_DEPTH)
    key_part = projected[:, expanded_dimension : 2 * expanded_dimension].reshape(
        -1, HEAD_TOTAL, HEAD_DEPTH
    )
    value_part = projected[:, 2 * expanded_dimension : 3 * expanded_dimension].reshape(
        -1, HEAD_TOTAL, HEAD_DEPTH
    )
    attended = attend(queries, key_part, value_part, keep_column, None).reshape(
        -1, expanded_dimension
    )
    sigmoid_scaled = (
        jax.nn.sigmoid(projected[:, 3 * expanded_dimension :].astype(jnp.float32)) * attended
    ).astype(jnp.bfloat16)
    mixed = column.astype(jnp.float32) + jnp.dot(
        sigmoid_scaled, vertical_projector, preferred_element_type=jnp.float32
    )
    inner = jnp.maximum(
        jnp.dot(
            layer_norm(mixed).astype(jnp.bfloat16),
            expansion_matrix,
            preferred_element_type=jnp.float32,
        ),
        0.0,
    ).astype(jnp.bfloat16)
    return (mixed + jnp.dot(inner, contraction_matrix, preferred_element_type=jnp.float32)).astype(
        jnp.bfloat16
    )


def body(
    homolog_tensor,
    pair_features,
    entry_real_mask,
    chain_ids,
    horizontal_matrices,
    horizontal_projector,
    bias_proj,
    chain_bias,
    column_proj,
    vertical_projector,
    expansion_matrix,
    contraction_matrix,
):
    row_count, local_residues, channels = homolog_tensor.shape
    expanded_dimension = HEAD_TOTAL * HEAD_DEPTH
    dap_count = lax.axis_size("dap")
    pair_rows, pair_columns, pair_width = pair_features.shape
    normed_pair = layer_norm(pair_features.astype(jnp.float32))
    projected_pair = jnp.einsum(
        "ijc,ch->hij", normed_pair, bias_proj, precision=lax.Precision.HIGHEST
    )
    row_chain = lax.dynamic_slice_in_dim(chain_ids, lax.axis_index("seq") * pair_rows, pair_rows)
    column_chain = lax.dynamic_slice_in_dim(
        chain_ids, lax.axis_index("dap") * pair_columns, pair_columns
    )
    same_chain = (row_chain[:, None] == column_chain[None, :]).astype(jnp.float32)
    chain_term = chain_bias[0][:, None, None] * same_chain + chain_bias[1][:, None, None] * (
        1.0 - same_chain
    )
    local_bias = (projected_pair + chain_term).astype(jnp.bfloat16)
    pair_bias = lax.all_gather(local_bias, "dap", axis=2, tiled=True)
    standardized = layer_norm(homolog_tensor.astype(jnp.float32)).astype(jnp.bfloat16)
    flat = standardized.reshape(-1, channels)
    keep_mask = entry_real_mask.astype(jnp.bfloat16)
    projected = (
        jnp.dot(flat, horizontal_matrices, preferred_element_type=jnp.float32)
        .astype(jnp.bfloat16)
        .reshape(row_count, local_residues, 4 * expanded_dimension)
    )
    queries = projected[..., :expanded_dimension]
    gating = projected[..., 3 * expanded_dimension :]
    key_values, keep_all = (
        lax.all_gather(
            projected[..., expanded_dimension : 3 * expanded_dimension], "seq", axis=1, tiled=True
        ),
        lax.all_gather(keep_mask, "seq", axis=1, tiled=True),
    )

    def one_row(inputs_row):
        row_queries, row_pairs, row_keep = inputs_row
        key_part = row_pairs[:, :expanded_dimension].reshape(-1, HEAD_TOTAL, HEAD_DEPTH)
        value_part = row_pairs[:, expanded_dimension:].reshape(-1, HEAD_TOTAL, HEAD_DEPTH)
        return attend(
            row_queries.reshape(local_residues, HEAD_TOTAL, HEAD_DEPTH),
            key_part,
            value_part,
            row_keep,
            pair_bias,
        ).reshape(local_residues, expanded_dimension)

    attended = lax.map(one_row, (queries, key_values, keep_all))
    sigmoid_scaled = (jax.nn.sigmoid(gating.astype(jnp.float32)) * attended).astype(jnp.bfloat16)
    row_result = jnp.dot(
        sigmoid_scaled.reshape(-1, expanded_dimension),
        horizontal_projector,
        preferred_element_type=jnp.float32,
    ).reshape(row_count, local_residues, channels)
    updated_rows = (homolog_tensor.astype(jnp.float32) + row_result).astype(jnp.bfloat16)
    per_device = local_residues // dap_count
    blocks = updated_rows.reshape(row_count, dap_count, per_device, channels)
    keep_blocks = keep_mask.reshape(row_count, dap_count, per_device)

    def single_column(inputs_col):
        return column_update(
            inputs_col[0],
            inputs_col[1],
            column_proj,
            vertical_projector,
            expansion_matrix,
            contraction_matrix,
        )

    column_block = lax.all_to_all(blocks, "dap", split_axis=1, concat_axis=0, tiled=True)
    column_keep = lax.all_to_all(keep_blocks, "dap", split_axis=1, concat_axis=0, tiled=True)
    inputs_col = (jnp.moveaxis(column_block[:, 0], 1, 0), jnp.moveaxis(column_keep[:, 0], 1, 0))
    output_list = lax.map(single_column, inputs_col)
    mixed = jnp.moveaxis(output_list, 0, 1)[:, None]
    returned = lax.all_to_all(mixed, "dap", split_axis=0, concat_axis=1, tiled=True)
    return returned.reshape(row_count, local_residues, channels)


LANES = 128
SUBLANES = 8
WAIT_FLOPS = 20_000_000_000
WHOLE_BYTES = 1 << 20
F32 = jnp.float32
BF16 = jnp.bfloat16


def mm(a, b):
    return lax.dot_general(a, b, (((1,), (0,)), ((), ())), preferred_element_type=F32)


def iota(shape, axis):
    return lax.broadcasted_iota(jnp.int32, shape, axis)


def normalize(parts, width):
    total = parts[0]
    for part in parts[1:]:
        total = total + part
    mean = jnp.sum(total, axis=-1, keepdims=True) * (1.0 / width)
    center = [part - mean for part in parts]
    total = center[0] * center[0]
    for part in center[1:]:
        total = total + part * part
    scale = lax.rsqrt(jnp.sum(total, axis=-1, keepdims=True) * (1.0 / width) + epsilon)
    return [part * scale for part in center]


def halves(x):
    return [x[:, k : k + LANES] for k in range(0, x.shape[1], LANES)]


def normalize_rows(x):
    return jnp.concatenate(normalize(halves(x), x.shape[1]), axis=1).astype(BF16)


def pack_kernel(*refs):
    count = (len(refs) - 2) // 2
    out_ref, arrived = refs[count], refs[-1]
    near = refs[count + 1 : -1]
    copies = [
        pltpu.make_async_copy(source, target, arrived.at[k])
        for k, (source, target) in enumerate(zip(refs[:count], near))
    ]
    for copy in copies:
        copy.start()
    for copy in copies:
        copy.wait()
    pair_ref, proj_ref, msa_ref, chain_ref, chain_bias_ref, mask_ref = near
    queries, keys, width = pair_ref.shape
    cells = HEAD_TOTAL * queries
    far, seq = lax.axis_index("far"), lax.axis_index("seq")
    dap = far * lax.axis_size("near") + lax.axis_index("near")
    pairs = queries * keys

    def spread_out(k, piece):
        out_ref[:, k] = jnp.broadcast_to(piece.astype(BF16)[None], (out_ref.shape[0], *piece.shape))

    block = jnp.concatenate(halves(msa_ref[0].astype(F32)), axis=0)
    last = block.shape[0] // keys
    for k in range(last):
        spread_out(far + k, block[k * keys : (k + 1) * keys])

    pair = pair_ref[...].astype(F32).reshape(pairs, width)
    center = pair - jnp.sum(pair, axis=-1, keepdims=True) * (1.0 / width)
    spread = jnp.sum(center * center, axis=-1, keepdims=True) * (1.0 / width)
    shape = (pairs, LANES)
    lane = iota(shape, 1)
    bias = jnp.zeros(shape, F32)
    for h in range(HEAD_TOTAL):
        projected = jnp.sum(center * proj_ref[h : h + 1, :], axis=-1, keepdims=True)
        bias = jnp.where(lane % cells // queries == h, projected, bias)
    bias = bias * lax.rsqrt(spread + epsilon)
    bias = jnp.where(lane % queries == iota(shape, 0) // keys, bias, 0.0)
    bias = jnp.sum(bias.reshape(pairs // SUBLANES, SUBLANES, LANES), axis=0)
    bias = bias + pltpu.roll(bias, keys, 0)

    shape = bias.shape
    row, lane = iota(shape, 0), iota(shape, 1)
    key_chain, query_chain = jnp.zeros(shape, jnp.int32), jnp.zeros(shape, jnp.int32)
    for k in range(keys):
        key_chain = jnp.where(row % keys == k, chain_ref[dap * keys + k], key_chain)
    for k in range(queries):
        query_chain = jnp.where(lane % queries == k, chain_ref[seq * queries + k], query_chain)
    same, other = jnp.zeros(shape, F32), jnp.zeros(shape, F32)
    for h in range(HEAD_TOTAL):
        here = lane % cells // queries == h
        same = jnp.where(here, chain_bias_ref[0, h], same)
        other = jnp.where(here, chain_bias_ref[1, h], other)
    mask = jnp.zeros(shape, F32)
    for k in range(SUBLANES):
        mask = jnp.where(row == k, mask_ref[0, k].astype(F32), mask)
    bias = bias + jnp.where(key_chain == query_chain, same, other)
    mask = jnp.where(lane == 0, mask, jnp.where(lane == 1, pltpu.roll(mask, keys, 0), 0.0))
    spread_out((1 - far) * last, jnp.where(lane >= cells, bias, mask)[:keys])


def block_kernel(
    seq_count, block_ref, row_proj_ref, row_out_ref, column_proj_ref, column_out_ref, expansion_ref,
    contraction_ref, out_ref, normed_ref, second_ref, one_ref,
):
    couples, pieces, own_rows, _ = block_ref.shape
    far_count, near_count = 2, couples // seq_count
    count = far_count * couples
    parts = (pieces - 1) // far_count
    width = parts * LANES
    members = far_count * near_count
    residues = seq_count * own_rows
    heads, depth = HEAD_TOTAL, HEAD_DEPTH
    inner = heads * depth
    cells = heads * own_rows
    tokens = members * own_rows
    seq = lax.axis_index("seq")
    me = lax.axis_index("near") * far_count + lax.axis_index("far")
    scaling = depth**-0.5

    def part(couple, far, k):
        return block_ref[couple, far * (parts + 1) + k].astype(F32)

    def tail(near, s):
        return block_ref[near * seq_count + s, parts].astype(F32)

    def mine(k):
        couple = [near * seq_count + seq for near in range(near_count)]
        return jnp.concatenate([part(n, far, k) for n in couple for far in range(far_count)], axis=0)

    def whole(k):
        both = [part(slice(None), far, k)[:, None] for far in range(far_count)]
        return jnp.concatenate(both, axis=1).reshape(count * own_rows, LANES)

    residual = [mine(k) for k in range(parts)]
    x = [whole(k) for k in range(parts)]
    normed = jnp.concatenate(normalize(x, width), axis=1).astype(BF16)
    normed_ref[...] = normed.reshape(near_count, seq_count, far_count * own_rows, width)
    own = normed_ref[:, seq].reshape(tokens, width)
    queries = mm(own, row_proj_ref[:, :inner]).astype(BF16).astype(F32)
    gates = mm(own, row_proj_ref[:, 3 * inner :]).astype(BF16).astype(F32)
    all_keys = mm(normed, row_proj_ref[:, inner : 2 * inner]).astype(BF16)
    all_values = mm(normed, row_proj_ref[:, 2 * inner : 3 * inner]).astype(BF16)

    head_of = iota((heads, 1, inner), 2) // depth == iota((heads, 1, inner), 0)
    spread = jnp.where(
        head_of[None], queries.reshape(members, 1, own_rows, inner), 0.0
    ).reshape(members * cells, inner).astype(BF16)

    shape = (own_rows, LANES)
    row, lane = iota(shape, 0), iota(shape, 1)
    lower = lane < cells
    bias = []
    first = row < own_rows // 2

    def swap(x):
        return pltpu.roll(x, own_rows // 2, 0)

    for far in range(far_count):
        for near in range(0, near_count, 2):
            even, odd = tail(near, seq), tail(near + 1, seq)
            both = jnp.where(first, swap(even), odd) if far else jnp.where(first, even, swap(odd))
            bias.append(jnp.where(lower, pltpu.roll(both, cells, 1), both))
    bias = jnp.concatenate(bias, axis=0)
    wide = iota((residues, LANES), 1) < cells
    taken = iota((LANES, 2 * LANES), 0) == iota((LANES, 2 * LANES), 1) // LANES
    masks = mm(block_ref[:, parts].reshape(couples * own_rows, LANES), taken.astype(F32).astype(BF16))
    masks = [half.reshape(couples, own_rows, LANES) for half in halves(masks)]
    masks = [(masks[0][n], masks[1][n]) for n in range(couples)]
    masks = [
        (jnp.where(first, one, swap(two)), jnp.where(first, swap(one), two)) for one, two in masks
    ]
    keeps = [
        jnp.concatenate(
            [jnp.where(lower, *masks[near * seq_count + s]) for s in range(seq_count)], axis=0
        ) > 0
        for near in range(near_count)
    ]

    def unmix(two):
        pieces = two.reshape(seq_count, far_count, own_rows, LANES)
        return jnp.where(wide, pieces[:, 0].reshape(wide.shape), pieces[:, 1].reshape(wide.shape))

    def remix(one):
        pieces = [
            half.reshape(seq_count, 1, own_rows, LANES)
            for half in (jnp.where(wide, one, 0.0), jnp.where(wide, 0.0, one))
        ]
        return jnp.concatenate(pieces, axis=1).reshape(2 * residues, LANES)

    scores = [
        lax.dot_general(
            all_keys[m * residues : (m + 2) * residues],
            spread[m * cells : (m + 2) * cells],
            (((1,), (1,)), ((), ())),
            preferred_element_type=F32,
        )
        for m in range(0, members, 2)
    ]
    scores = [unmix(two) * scaling + bias for two in scores]
    scores = [jnp.where(keep, two, -1000000000.0) for two, keep in zip(scores, keeps)]
    scores = [jnp.exp(two - jnp.max(two, axis=0, keepdims=True)) for two in scores]
    weights = [two * (1.0 / jnp.sum(two, axis=0, keepdims=True)) for two in scores]
    weights = [remix(two).astype(BF16) for two in weights]
    mixed = [
        lax.dot_general(
            two, all_values[2 * k * residues : 2 * (k + 1) * residues],
            (((0,), (0,)), ((), ())), preferred_element_type=F32,
        )
        for k, two in enumerate(weights)
    ]
    mixed = [
        jnp.sum(jnp.where(head_of[None], two.reshape(2, heads, own_rows, inner), 0.0), axis=1)
        for two in mixed
    ]
    attended = jnp.concatenate(mixed, axis=0).reshape(tokens, inner)
    gated = (jax.nn.sigmoid(gates) * attended).astype(BF16)
    one = (jnp.concatenate(residual, axis=1) + mm(gated, row_out_ref[...])).astype(BF16).astype(F32)
    one_ref[...] = one.reshape(members, own_rows, width)

    second = normalize_rows(one)
    second_ref[...] = second.reshape(members, own_rows, width)
    key_values = mm(second, column_proj_ref[:, inner : 3 * inner]).astype(BF16).astype(F32)
    own = second_ref[me]
    queries = mm(own, column_proj_ref[:, :inner]).astype(BF16).astype(F32)
    gates = mm(own, column_proj_ref[:, 3 * inner :]).astype(BF16).astype(F32)
    products = (
        key_values[:, :inner].reshape(members, own_rows, inner) * queries[None]
    ).reshape(tokens, inner)
    high = products.astype(BF16)
    low = (products - high.astype(F32)).astype(BF16)
    same_head = (iota((inner, inner), 0) // depth == iota((inner, inner), 1) // depth).astype(
        F32
    ).astype(BF16)
    scores = (mm(high, same_head) + mm(low, same_head)) * scaling
    scores = scores.reshape(members, own_rows, inner)
    keep = []
    for m in range(members):
        couple, far = m // far_count * seq_count, m % far_count
        mask = masks[couple][far]
        for s in range(1, seq_count):
            mask = jnp.where(seq == s, masks[couple + s][far], mask)
        keep.append(jnp.concatenate([mask] * (inner // LANES), axis=1)[None])
    keep = jnp.concatenate(keep, axis=0)
    scores = jnp.where(keep > 0, scores, -1000000000.0)
    scores = jnp.exp(scores - jnp.max(scores, axis=0, keepdims=True))
    weights = (scores * (1.0 / jnp.sum(scores, axis=0, keepdims=True))).astype(BF16).astype(F32)
    attended = jnp.sum(
        weights * key_values[:, inner:].reshape(members, own_rows, inner), axis=0
    )
    gated = (jax.nn.sigmoid(gates) * attended).astype(BF16)
    two = one_ref[me] + mm(gated, column_out_ref[...])
    hidden = jnp.maximum(mm(normalize_rows(two), expansion_ref[...]), 0.0).astype(BF16)
    out_ref[0] = (two + mm(hidden, contraction_ref[...])).astype(BF16)


def whole_body(
    homolog_tensor,
    pair_features,
    entry_real_mask,
    chain_ids,
    horizontal_matrices,
    horizontal_projector,
    bias_proj,
    chain_bias,
    column_proj,
    vertical_projector,
    expansion_matrix,
    contraction_matrix,
):
    _, own_rows, width = homolog_tensor.shape
    seq_count = lax.axis_size("seq")
    dap_count = lax.axis_size("far") * lax.axis_size("near")
    count = dap_count * seq_count
    rows = own_rows // 2
    pieces = 2 * width // LANES + 1
    vmem, hbm = (pl.BlockSpec(memory_space=space) for space in (pltpu.VMEM, pltpu.HBM))
    vectors = [pair_features, bias_proj.T, homolog_tensor]
    scalars = [chain_ids, chain_bias, entry_real_mask]
    packed = pl.pallas_call(
        pack_kernel,
        out_shape=jax.ShapeDtypeStruct((count, pieces, rows, LANES), BF16),
        in_specs=[hbm] * len(vectors + scalars),
        out_specs=vmem,
        scratch_shapes=[
            *(pltpu.VMEM(operand.shape, operand.dtype) for operand in vectors),
            *(pltpu.SMEM(operand.shape, operand.dtype) for operand in scalars),
            pltpu.SemaphoreType.DMA((len(vectors + scalars),)),
        ],
        compiler_params=pltpu.CompilerParams(vmem_limit_bytes=8 << 20),
        cost_estimate=pl.CostEstimate(flops=WAIT_FLOPS, bytes_accessed=count * pieces * rows * LANES * 2, transcendentals=0),
    )(*map(in_hbm, vectors + scalars))
    blocks = lax.all_to_all(packed, ("near", "seq", "far"), split_axis=0, concat_axis=0, tiled=True)
    blocks = blocks.reshape(count // 2, pieces, 2 * rows, LANES)
    return pl.pallas_call(
        functools.partial(block_kernel, seq_count),
        out_shape=jax.ShapeDtypeStruct(homolog_tensor.shape, BF16),
        in_specs=[vmem] * 7,
        out_specs=vmem,
        scratch_shapes=[
            pltpu.VMEM((dap_count // 2, seq_count, 2 * own_rows, width), BF16),
            pltpu.VMEM((dap_count, own_rows, width), BF16),
            pltpu.VMEM((dap_count, own_rows, width), F32),
        ],
        compiler_params=pltpu.CompilerParams(vmem_limit_bytes=16 << 20),
    )(
        blocks,
        horizontal_matrices,
        horizontal_projector,
        column_proj,
        vertical_projector,
        expansion_matrix,
        contraction_matrix,
    )


def in_hbm(operand):
    return pltpu.with_memory_space_constraint(operand, pltpu.HBM)


def fits_whole(homolog_tensor, pair_features, dap_count, seq_count):
    rows, residues, width = homolog_tensor.shape
    _, _, pair_width = pair_features.shape
    return (
        rows == dap_count
        and residues == seq_count * SUBLANES
        and 2 * residues == dap_count * SUBLANES
        and dap_count % 4 == 0
        and 2 * HEAD_TOTAL * SUBLANES == LANES
        and width % LANES == 0
        and pair_width == LANES
        and HEAD_TOTAL * HEAD_DEPTH % LANES == 0
        and homolog_tensor.size * 2 <= WHOLE_BYTES
    )


def solution(mesh):
    def placed(dap):
        return (P(dap, "seq", None), P("seq", dap, None), P(dap, "seq"), *[P()] * 9)

    def step(*operands):
        dap_count, seq_count = mesh.shape["dap"], mesh.shape["seq"]
        if fits_whole(operands[0], operands[1], dap_count, seq_count):
            devices = mesh.devices.reshape(2, dap_count // 2, seq_count)
            used, chosen, dap = Mesh(devices, ("far", "near", "seq")), whole_body, ("far", "near")
        else:
            used, chosen, dap = mesh, body, "dap"
        return jax.shard_map(
            chosen, mesh=used, in_specs=placed(dap), out_specs=P(dap, "seq", None), check_vma=False
        )(*operands)

    return step
```
